512 devices in a mesh: rep: 16 (over z), gx: 4 (over x_lo, core), gy: 8 (over y, x_hi).
Axes of the slice: x: 4 (x_hi: 2, x_lo: 2; x = x_hi * 2 + x_lo), y: 4, z: 16, core: 2. Of those that a mesh axis runs over, the one named last changes fastest.
Arguments:
- velocity: bfloat16 [16, 128, 256, 128], P('rep', 'gx', 'gy'), may hold values from -1.5 to 1.5
- tracers: bfloat16 [16, 128, 256, 128], P('rep', 'gx', 'gy'), may hold values from 0.5 to 2
- forcing: bfloat16 [48, 128, 256, 128], P('rep', 'gx', 'gy'), may hold values from -6 to 6
- coefficients: float32 [48], P('rep'), may hold values from -1.2 to 1.2
- land_mask: int32 [128, 256], P('gx', 'gy'), may hold values 0 or 1
- step_levels: int32 [3], replicated, may hold values from 0 to 15
Outputs:
- combined: float32 [128, 256, 128], P(('gx', 'rep'), 'gy')
- adjoints: float32 [48, 128, 256, 128], P('rep', 'gx', 'gy')
The draws below stay inside these ranges and needn't reach their ends.
Inputs may be any that keep to these rules, and one draw needn't show every extreme that they name: `step_levels`: each entry names the group along rep that stores the level.
All inputs are finite; a program needn't handle non-finite values. No bound on the sum of `land_mask` on one device may be relied on, other than what follows from the above.
Results may differ from the reference program's by a relative error of at most 0.0003.
Values may be sent and summed in bfloat16 or wider, within the bound.
No kernel may reach another device: no remote copies, remote signals or barrier semaphores. Data moves between devices by JAX's collectives and lax.ppermute only.
A program may use at most 64 MiB of HBM per device.

```python
import math
import jax
import jax.numpy as jnp
from jax import lax

NZ = 64
STEPS = 3
REPS = 48
NX = 128
NY = 256
LEVELS = 16
N_REP = 16


def set_ends(values, own_key, smallest, largest):
    extent = values.shape
    place = [jax.random.randint(jax.random.fold_in(own_key, axis), (), 0, extent[axis]) for axis in range(len(extent))]
    values = values.at[tuple(place)].set(smallest)
    longest = extent.index(max(extent))
    place[longest] = (place[longest] + 1) % extent[longest]
    return values.at[tuple(place)].set(largest)


def steps_of(own_key, extent, shards, low, largest):
    gain, own = 1.0, jax.random.fold_in(own_key, 6)
    for position, blocks in shards:
        steps = jnp.exp(jax.random.uniform(jax.random.fold_in(own, position), (blocks,), jnp.float32, low / len(shards), largest / len(shards)))
        gain = gain * jnp.repeat(steps, extent[position] // blocks).reshape([-1 if axis == position else 1 for axis in range(len(extent))])
    return gain


def gaussian(rng, dims, scale, bound, split=(), held_as=jnp.bfloat16):
    drawn = scale * jax.random.normal(rng, dims, jnp.float32)
    if split:
        drawn = drawn * steps_of(rng, dims, split, -0.22, 0.18)
    return jnp.clip(drawn, -bound, bound).astype(held_as)


def setup_inputs(seed: int = 0) -> dict:
    splits = jax.random.split(jax.random.key(seed), 7)
    velocity = jnp.clip(jax.random.uniform(splits[0], (LEVELS, NX, NY, 2 * NZ), jnp.float32, -1.5, 1.5) * steps_of(splits[0], (LEVELS, NX, NY, 2 * NZ), ((0, 16), (1, 4), (2, 8)), -0.4, 0.0), -1.5, 1.5).astype(jnp.bfloat16)
    tracers = jnp.clip(jnp.exp(math.log(2.0) - 1.3862944 * jax.random.uniform(splits[1], (LEVELS, NX, NY, 2 * NZ), jnp.float32) ** steps_of(splits[1], (LEVELS, NX, NY, 2 * NZ), ((0, 16), (1, 4), (2, 8)), -0.2, 0.2)), 0.5, 2.0).astype(jnp.bfloat16)
    forcing = gaussian(splits[2], (REPS, NX, NY, 2 * NZ), 1.0, 6.0, ((0, 16), (1, 4), (2, 8)))
    coefficients = gaussian(splits[3], (REPS,), 0.2, 1.2, ((0, 16),), jnp.float32)
    land_mask = set_ends((jax.random.randint(splits[4], (NX, NY), 0, 8) < 7).astype(jnp.int32), jax.random.fold_in(splits[4], 1), 0, 1)
    step_levels = jax.random.randint(splits[5], (STEPS,), 0, N_REP).astype(jnp.int32)
    return {"velocity": velocity, "tracers": tracers, "forcing": forcing, "coefficients": coefficients, "land_mask": land_mask, "step_levels": step_levels}


time_step = 0.1


def advance(state, speed, tracer, ocean):
    half = state.shape[-1] // 2
    along_x = jnp.concatenate([speed[..., :half], speed[..., :half]], axis=-1)
    along_y = jnp.concatenate([speed[..., half:], speed[..., half:]], axis=-1)
    east = jnp.pad(along_x * state, ((1, 1), (1, 1), (0, 0)))
    north = jnp.pad(along_y * state, ((1, 1), (1, 1), (0, 0)))
    padded = jnp.pad(state, ((1, 1), (1, 1), (0, 0)))
    advect = 0.5 * (east[:-2, 1:-1] - east[2:, 1:-1]) + 0.5 * (north[1:-1, :-2] - north[1:-1, 2:])
    spread = padded[:-2, 1:-1] + padded[2:, 1:-1] + padded[1:-1, :-2] + padded[1:-1, 2:] - 4.0 * state
    mixing = tracer[..., :half] * state[..., :half] - tracer[..., half:] * state[..., half:]
    exchange = jnp.concatenate([-mixing, mixing], axis=-1)
    return ocean * (state + time_step * (advect + spread + exchange))


def reference(velocity, tracers, forcing, coefficients, land_mask, step_levels):
    ocean = land_mask.astype(jnp.float32)[:, :, None]
    speeds = velocity[step_levels].astype(jnp.float32)
    tracer_levels = tracers[step_levels].astype(jnp.float32)

    def one(total, item):
        force, weight = item
        state = force.astype(jnp.float32)
        for step in range(STEPS):
            state = advance(state, speeds[step], tracer_levels[step], ocean)
        return total + weight * state, state

    start = jnp.zeros(forcing.shape[1:], jnp.float32)
    total, adjoints = lax.scan(one, start, (forcing, coefficients))
    return total, adjoints
```

```python
import functools

import jax
import jax.numpy as jnp
from jax import lax
from jax.experimental import pallas as pl
from jax.experimental.pallas import tpu as pltpu
from jax.sharding import PartitionSpec as P

F32 = jnp.float32
BF16 = jnp.bfloat16
STEPS = 3
REACH = 3
WIDE = 40
SCALE = 2.0**15
DT = 0.1

LEVEL_HALO = ((0, 0, 3), (1, 0, 2), (0, 1, 2), (1, 1, 1), (0, 2, 1))


def x_index(reps):
    table, at = {}, 0
    for r in range(reps):
        table["f", r] = (at, REACH)
        at += REACH
    for which, level, width in LEVEL_HALO:
        table[which, level] = (at, width)
        at += width
    return table, at


def y_index(reps):
    keys = [("f", r) for r in range(reps)] + [(w, k) for w, k, _ in LEVEL_HALO]
    width = {("f", r): REACH for r in range(reps)}
    width.update({(w, k): n for w, k, n in LEVEL_HALO})
    strips = [(key, d) for key in keys for d in range(1, width[key] + 1)]
    corners = [
        (key, d, e, side)
        for key in keys
        for d in range(1, width[key])
        for e in range(1, width[key] - d + 1)
        for side in (0, 1)
    ]
    return strips, corners


def level_row(lev_ref, which, level, x):
    return lev_ref[x // 2, level, 2 * which + lax.rem(x, 2)]


def pack_kernel(reps, rows, cols, f_ref, lev_ref, up_ref, down_ref, left_ref, right_ref, tile, out):
    xi, _ = x_index(reps)
    strips, corners = y_index(reps)
    keys = []
    for key, _ in strips:
        if key not in keys:
            keys.append(key)
    base = len(strips) * rows
    for side, target in ((0, left_ref), (1, right_ref)):
        lo = 0 if side == 0 else cols - 8
        for key in keys:
            for x in range(rows):
                if key[0] == "f":
                    v = f_ref[key[1], x, lo : lo + 8, :]
                else:
                    v = lev_ref[x // 2, key[1], 2 * key[0] + x % 2, lo : lo + 8, :]
                tile[pl.ds(x * 8, 8), :] = v.astype(F32)
            for n, (k, d) in enumerate(strips):
                if k == key:
                    c = d - 1 if side == 0 else 8 - d
                    target[pl.ds(n * rows, rows), :] = tile[pl.ds(c, rows, stride=8), :].astype(target.dtype)
        out[...] = jnp.zeros_like(out)
        for n, (key, d, e, edge) in enumerate(corners):
            first, width = xi[key]
            row = up_ref[first + width - e, lo : lo + 8, :] if edge == 0 else down_ref[first + e - 1, lo : lo + 8, :]
            c = d - 1 if side == 0 else 8 - d
            out[pl.ds(n, 1), :] = row.astype(F32)[c : c + 1]
        target[pl.ds(base, out.shape[0]), :] = out[...].astype(target.dtype)


def steps_kernel(
    reps, rows, cols,
    coef_ref, f_ref, lev_ref, up_ref, down_ref, left_ref, right_ref,
    adj_ref, sum_ref,
    state, vx, vy, keep, swap, spare,
):
    xi, _ = x_index(reps)
    strips, corners = y_index(reps)
    total = rows + 2 * REACH
    base = len(strips) * rows
    half = 64
    spare_rows = spare.shape[0]

    def fill(target, key, main):
        def body(x, carry):
            target[pl.ds(pl.multiple_of((x + REACH) * WIDE, 8), cols), :] = main(x).astype(F32)
            return carry

        lax.fori_loop(0, rows, body, 0, unroll=4)
        first, width = xi[key]
        for e in range(1, width + 1):
            target[pl.ds((REACH - e) * WIDE, cols), :] = up_ref[first + width - e].astype(F32)
            target[pl.ds((REACH + rows + e - 1) * WIDE, cols), :] = down_ref[first + e - 1].astype(F32)
        for side, source in ((0, left_ref), (1, right_ref)):
            for n, (k, d) in enumerate(strips):
                if k == key:
                    c = WIDE - d if side == 0 else cols + d - 1
                    target[pl.ds(REACH * WIDE + c, rows, stride=WIDE), :] = source[pl.ds(n * rows, rows), :].astype(F32)
            mine = [(n, q) for n, q in enumerate(corners) if q[0] == key]
            for n, (_, d, e, edge) in mine:
                c = WIDE - d if side == 0 else cols + d - 1
                x = REACH - e if edge == 0 else REACH + rows + e - 1
                target[pl.ds(x * WIDE + c, 1), :] = spare[pl.ds(side * (spare_rows // 2) + n, 1), :]

    for side, source in ((0, left_ref), (1, right_ref)):
        spare[pl.ds(side * (spare_rows // 2), spare_rows // 2), :] = source[pl.ds(base, spare_rows // 2), :].astype(F32)

    for r in range(reps):
        fill(state.at[0, r], ("f", r), lambda x, r=r: f_ref[r, x])

    lane = lax.broadcasted_iota(jnp.int32, (WIDE, 128), 1)
    low = lane < half
    for k in range(STEPS):
        now, later = k % 2, (k + 1) % 2
        fill(vx, (0, k), lambda x, k=k: level_row(lev_ref, 0, k, x))
        if k < STEPS - 1:
            fill(keep, (1, k), lambda x, k=k: level_row(lev_ref, 1, k, x))
        else:

            def body3(x, carry):
                keep[pl.ds(pl.multiple_of((x + REACH) * WIDE, 8), cols), :] = level_row(lev_ref, 1, STEPS - 1, x).astype(F32)
                return carry

            lax.fori_loop(0, rows, body3, 0, unroll=4)

        def coefficients(x, carry):
            at = pl.ds(pl.multiple_of(x * WIDE, 8), WIDE)
            v = vx[at, :] * (0.5 * DT / SCALE)
            t = keep[at, :]
            o = pltpu.roll(v, half, axis=1)
            vx[at, :] = jnp.where(low, v, o)
            vy[at, :] = jnp.where(low, o, v)
            keep[at, :] = jnp.where(t > 0.0, (1.0 - 4.0 * DT) - DT * t, 4.0)
            swap[at, :] = DT * pltpu.roll(t, half, axis=1)
            return carry

        lax.fori_loop(k, total - k, coefficients, 0)

        def row(x, carry):
            at = pl.ds(pl.multiple_of(x * WIDE, 8), WIDE)
            above = pl.ds(pl.multiple_of((x - 1) * WIDE, 8), WIDE)
            below = pl.ds(pl.multiple_of((x + 1) * WIDE, 8), WIDE)
            a = DT + vx[above, :]
            b = DT - vx[below, :]
            y = vy[at, :]
            c, d = DT + y, DT - y
            centre = keep[at, :]
            other = swap[at, :]
            ocean = centre < 1.0
            weighted = None
            for r in range(reps):
                s = state[now, r, at, :]
                new = (
                    a * state[now, r, above, :]
                    + b * state[now, r, below, :]
                    + pltpu.roll(c * s, 1, axis=0)
                    + pltpu.roll(d * s, WIDE - 1, axis=0)
                    + centre * s
                    + other * pltpu.roll(s, half, axis=1)
                )
                new = jnp.where(ocean, new, 0.0)
                if k < STEPS - 1:
                    state[later, r, at, :] = new
                else:
                    own = new[:cols]
                    adj_ref[r, x - REACH] = own
                    part = coef_ref[r] * own
                    weighted = part if weighted is None else weighted + part
            if k == STEPS - 1:
                sum_ref[x - REACH] = weighted
            return carry

        lax.fori_loop(k + 1, total - k - 1, row, 0)


def shift(x, axis, by):
    n = lax.axis_size(axis)
    if by > 0:
        return lax.ppermute(x, axis, [(i, i + 1) for i in range(n - 1)])
    return lax.ppermute(x, axis, [(i + 1, i) for i in range(n - 1)])


def local(velocity, tracers, forcing, coefficients, land_mask, step_levels):
    groups = lax.axis_size("rep")
    reps, rows, cols, lanes = forcing.shape
    own = rows // groups
    ocean = (land_mask > 0)[:, :, None]
    tracer = jnp.where(ocean, tracers[0], jnp.zeros_like(tracers[0]))
    speed = velocity[0] * BF16(SCALE)
    mine = jnp.concatenate([speed.reshape(groups, own, cols, lanes), tracer.reshape(groups, own, cols, lanes)], axis=1)
    slices = lax.all_to_all(mine, "rep", 0, 0, tiled=True)
    picked = jnp.stack([lax.dynamic_index_in_dim(slices, step_levels[k], 0, False) for k in range(STEPS)])
    lev = lax.all_gather(picked.astype(jnp.float16), "rep", axis=0, tiled=False)
    lev = lax.optimization_barrier(lev).astype(BF16)

    def edge(rows_of, source):
        return [source[x // own, k, which * own + x % own] for which, k, x in rows_of]

    last, first = [], []
    for which, k, width in LEVEL_HALO:
        last += [(which, k, rows - width + i) for i in range(width)]
        first += [(which, k, i) for i in range(width)]
    to_down = jnp.concatenate([forcing[:, rows - REACH :].reshape(-1, cols, lanes), jnp.stack(edge(last, lev))])
    to_up = jnp.concatenate([forcing[:, :REACH].reshape(-1, cols, lanes), jnp.stack(edge(first, lev))])
    up = shift(to_down, "gx", 1)
    down = shift(to_up, "gx", -1)

    strips, corners = y_index(reps)
    extra = -(-len(corners) // 16) * 16
    length = len(strips) * rows + extra
    payload = jax.ShapeDtypeStruct((length, lanes), BF16)
    to_left, to_right = pl.pallas_call(
        functools.partial(pack_kernel, reps, rows, cols),
        out_shape=(payload, payload),
        scratch_shapes=[pltpu.VMEM((rows * 8, lanes), F32), pltpu.VMEM((extra, lanes), F32)],
        name="pack",
    )(forcing, lev, up, down)
    right = shift(to_left, "gy", -1)
    left = shift(to_right, "gy", 1)

    vm = pl.BlockSpec(memory_space=pltpu.VMEM)
    size = (rows + 2 * REACH) * WIDE
    adjoints, weighted = pl.pallas_call(
        functools.partial(steps_kernel, reps, rows, cols),
        out_shape=(
            jax.ShapeDtypeStruct((reps, rows, cols, lanes), F32),
            jax.ShapeDtypeStruct((rows, cols, lanes), F32),
        ),
        in_specs=[pl.BlockSpec(memory_space=pltpu.SMEM)] + [vm] * 6,
        out_specs=(vm, vm),
        scratch_shapes=[pltpu.VMEM((2, reps, size, lanes), F32)]
        + [pltpu.VMEM((size, lanes), F32)] * 4
        + [pltpu.VMEM((2 * extra, lanes), F32)],
        name="steps",
    )(coefficients, forcing, lev, up, down, left, right)

    parts = lax.all_to_all(weighted.reshape(groups, own, cols, lanes), "rep", 0, 0, tiled=True)
    return jnp.sum(parts, axis=0), adjoints


def solution(mesh):
    placed = (
        P("rep", "gx", "gy", None),
        P("rep", "gx", "gy", None),
        P("rep", "gx", "gy", None),
        P("rep"),
        P("gx", "gy"),
        P(),
    )
    return jax.shard_map(
        local,
        mesh=mesh,
        in_specs=placed,
        out_specs=(P(("gx", "rep"), "gy", None), P("rep", "gx", "gy", None)),
        check_vma=False,
    )
```

```python
import functools

import jax
import jax.numpy as jnp
from jax import lax
from jax.experimental import pallas as pl
from jax.experimental.pallas import tpu as pltpu
from jax.sharding import PartitionSpec as P

F32 = jnp.float32
BF16 = jnp.bfloat16
STEPS = 3
REACH = 3
WIDE = 40
SCALE = 2.0**15
DT = 0.1

LEVEL_HALO = ((0, 0, 3), (1, 0, 2), (0, 1, 2), (1, 1, 1), (0, 2, 1))


def x_index(reps):
    table, at = {}, 0
    for r in range(reps):
        table["f", r] = (at, REACH)
        at += REACH
    for which, level, width in LEVEL_HALO:
        table[which, level] = (at, width)
        at += width
    return table, at


def y_index(reps):
    keys = [("f", r) for r in range(reps)] + [(w, k) for w, k, _ in LEVEL_HALO]
    width = {("f", r): REACH for r in range(reps)}
    width.update({(w, k): n for w, k, n in LEVEL_HALO})
    strips = [(key, d) for key in keys for d in range(1, width[key] + 1)]
    corners = [
        (key, d, e, side)
        for key in keys
        for d in range(1, width[key])
        for e in range(1, width[key] - d + 1)
        for side in (0, 1)
    ]
    return strips, corners


def pack_kernel(reps, rows, cols, f_ref, lev_ref, up_ref, down_ref, left_ref, right_ref, tile, out):
    xi, _ = x_index(reps)
    strips, corners = y_index(reps)
    keys = []
    for key, _ in strips:
        if key not in keys:
            keys.append(key)
    base = len(strips) * rows
    for side, target in ((0, left_ref), (1, right_ref)):
        lo = 0 if side == 0 else cols - 8
        for key in keys:
            for x in range(rows):
                if key[0] == "f":
                    v = f_ref[key[1], x, lo : lo + 8, :]
                else:
                    v = lev_ref[x // 2, key[1], 2 * key[0] + x % 2, lo : lo + 8, :]
                tile[pl.ds(x * 8, 8), :] = v.astype(F32)
            for n, (k, d) in enumerate(strips):
                if k == key:
                    c = d - 1 if side == 0 else 8 - d
                    target[pl.ds(n * rows, rows), :] = tile[pl.ds(c, rows, stride=8), :].astype(target.dtype)
        out[...] = jnp.zeros_like(out)
        for n, (key, d, e, edge) in enumerate(corners):
            first, width = xi[key]
            row = up_ref[first + width - e, lo : lo + 8, :] if edge == 0 else down_ref[first + e - 1, lo : lo + 8, :]
            c = d - 1 if side == 0 else 8 - d
            out[pl.ds(n, 1), :] = row.astype(F32)[c : c + 1]
        target[pl.ds(base, out.shape[0]), :] = out[...].astype(target.dtype)


def own_kernel(groups, own, v_hbm, t_hbm, mask_hbm, out, v_ref, t_ref, mask_ref, sems):
    copies = [
        pltpu.make_async_copy(source, target, sems.at[n])
        for n, (source, target) in enumerate(((mask_hbm, mask_ref), (v_hbm, v_ref), (t_hbm, t_ref)))
    ]
    for copy in copies:
        copy.start()
    copies[0].wait()
    ocean = jnp.transpose(mask_ref[...].astype(F32))
    copies[1].wait()
    for x in range(groups * own):
        out[x // own, x % own] = v_ref[0, x] * BF16(SCALE)
    copies[2].wait()
    for x in range(groups * own):
        t = t_ref[0, x].astype(F32)
        out[x // own, own + x % own] = jnp.where(ocean[:, x : x + 1] > 0.0, t, 0.0).astype(BF16)


def pick_kernel(levels_ref, slices_ref, out):
    for k in range(STEPS):
        out[k] = slices_ref[levels_ref[k]]


def steps_kernel(
    reps, rows, cols,
    coef_ref, f_ref, lev_ref, up_ref, down_ref, left_ref, right_ref,
    adj_hbm, sum_ref,
    state, vx, vy, keep, swap, spare, adj_ref, sems,
):
    xi, _ = x_index(reps)
    strips, corners = y_index(reps)
    total = rows + 2 * REACH
    base = len(strips) * rows
    half = 64
    extra = spare.shape[0] // 2

    def put_state(r):
        def put(at, v):
            state[0, r, at, :] = v

        return put

    def put_speed(at, v):
        v = v * (0.5 * DT / SCALE)
        o = pltpu.roll(v, half, axis=1)
        is_low = lax.broadcasted_iota(jnp.int32, v.shape, 1) < half
        vx[at, :] = jnp.where(is_low, v, o)
        vy[at, :] = jnp.where(is_low, o, v)

    def put_tracer(at, t):
        keep[at, :] = jnp.where(t > 0.0, (1.0 - 4.0 * DT) - DT * t, 4.0)
        swap[at, :] = DT * pltpu.roll(t, half, axis=1)

    def fill(put, key):
        if key in xi:
            first, width = xi[key]
            for e in range(1, width + 1):
                put(pl.ds((REACH - e + 1) * WIDE, cols), up_ref[first + width - e].astype(F32))
                put(pl.ds((REACH + rows + e) * WIDE, cols), down_ref[first + e - 1].astype(F32))
        for side, source in ((0, left_ref), (1, right_ref)):
            for n, (k, d) in enumerate(strips):
                if k == key:
                    c = -d if side == 0 else cols + d - 1
                    at = pl.ds((REACH + 1) * WIDE + c, rows, stride=WIDE)
                    put(at, source[pl.ds(n * rows, rows), :].astype(F32))
            for n, (k, d, e, edge) in enumerate(corners):
                if k == key:
                    c = -d if side == 0 else cols + d - 1
                    x = REACH - e if edge == 0 else REACH + rows + e - 1
                    put(pl.ds((x + 1) * WIDE + c, 1), spare[pl.ds(side * extra + n, 1), :])

    spare[pl.ds(0, extra), :] = left_ref[pl.ds(base, extra), :].astype(F32)
    spare[pl.ds(extra, extra), :] = right_ref[pl.ds(base, extra), :].astype(F32)

    def forcing_row(x, carry):
        at = pl.ds(pl.multiple_of((x + REACH + 1) * WIDE, 8), cols)
        for r in range(reps):
            state[0, r, at, :] = f_ref[r, x].astype(F32)
        return carry

    lax.fori_loop(0, rows, forcing_row, 0, unroll=4)
    for r in range(reps):
        fill(put_state(r), ("f", r))

    for k in range(STEPS):
        now, later = k % 2, (k + 1) % 2

        def level_rows(g, carry, k=k):
            own = lev_ref.shape[2] // 2
            for i in range(own):
                at = pl.ds(pl.multiple_of((g * own + i + REACH + 1) * WIDE, 8), cols)
                put_speed(at, lev_ref[g, k, i].astype(F32))
                put_tracer(at, lev_ref[g, k, own + i].astype(F32))
            return carry

        lax.fori_loop(0, lev_ref.shape[0], level_rows, 0)
        fill(put_speed, (0, k))
        fill(put_tracer, (1, k))

        def row(x, carry, k=k, now=now, later=later):
            start = pl.multiple_of(x * WIDE, 8)
            for j in range(0, cols if k == STEPS - 1 else WIDE, 8):
                at = pl.ds(start + j, 8)
                above, below = pl.ds(start + j - WIDE, 8), pl.ds(start + j + WIDE, 8)
                before, after = pl.ds(start + j - 1, 8), pl.ds(start + j + 1, 8)
                a = DT + vx[above, :]
                b = DT - vx[below, :]
                c = DT + vy[before, :]
                d = DT - vy[after, :]
                centre = keep[at, :]
                other = swap[at, :]
                ocean = centre < 1.0
                weighted = None
                for r in range(reps):
                    s = state[now, r, at, :]
                    new = (
                        (a * state[now, r, above, :] + b * state[now, r, below, :])
                        + (c * state[now, r, before, :] + d * state[now, r, after, :])
                        + (centre * s + other * pltpu.roll(s, half, axis=1))
                    )
                    new = jnp.where(ocean, new, 0.0)
                    if k < STEPS - 1:
                        state[later, r, at, :] = new
                    else:
                        adj_ref[r, x - REACH - 1, pl.ds(j, 8)] = new
                        part = coef_ref[r] * new
                        weighted = part if weighted is None else weighted + part
                if k == STEPS - 1:
                    sum_ref[x - REACH - 1, pl.ds(j, 8)] = weighted
            return carry

        if k < STEPS - 1:
            lax.fori_loop(k + 1, total - k, row, 0)

    stretch = rows // sems.shape[0]

    def out_copy(g):
        at = pl.ds(g * stretch, stretch)
        return pltpu.make_async_copy(adj_ref.at[:, at], adj_hbm.at[:, at], sems.at[g])

    def some_rows(g, carry):
        lax.fori_loop(REACH + 1 + g * stretch, REACH + 1 + (g + 1) * stretch, row, 0)
        out_copy(g).start()
        return carry

    lax.fori_loop(0, sems.shape[0], some_rows, 0)
    for g in range(sems.shape[0]):
        out_copy(g).wait()


def shift(x, axis, by):
    n = lax.axis_size(axis)
    if by > 0:
        return lax.ppermute(x, axis, [(i, i + 1) for i in range(n - 1)])
    return lax.ppermute(x, axis, [(i + 1, i) for i in range(n - 1)])


def local(velocity, tracers, forcing, coefficients, land_mask, step_levels):
    groups = lax.axis_size("rep")
    reps, rows, cols, lanes = forcing.shape
    own = rows // groups
    hbm = pl.BlockSpec(memory_space=pltpu.HBM)
    mine = pl.pallas_call(
        functools.partial(own_kernel, groups, own),
        out_shape=jax.ShapeDtypeStruct((groups, 2 * own, cols, lanes), BF16),
        in_specs=[hbm] * 3,
        scratch_shapes=[
            pltpu.VMEM(velocity.shape, BF16),
            pltpu.VMEM(tracers.shape, BF16),
            pltpu.VMEM(land_mask.shape, land_mask.dtype),
            pltpu.SemaphoreType.DMA((3,)),
        ],
        compiler_params=pltpu.CompilerParams(vmem_limit_bytes=8 * 2**20),
        name="own",
    )(velocity, tracers, land_mask)
    slices = lax.all_to_all(mine, "rep", 0, 0, tiled=True)
    slices, forcing, step_levels = lax.optimization_barrier((slices, forcing, step_levels))
    picked = pl.pallas_call(
        pick_kernel,
        out_shape=jax.ShapeDtypeStruct((STEPS, 2 * own, cols, lanes), BF16),
        in_specs=[pl.BlockSpec(memory_space=pltpu.SMEM), pl.BlockSpec(memory_space=pltpu.VMEM)],
        compiler_params=pltpu.CompilerParams(vmem_limit_bytes=8 * 2**20),
        name="pick",
    )(step_levels, slices)
    lev = lax.all_gather(picked.astype(jnp.float16), "rep", axis=0, tiled=False)
    lev = lax.optimization_barrier(lev).astype(BF16)

    def edge(rows_of, source):
        return [source[x // own, k, which * own + x % own] for which, k, x in rows_of]

    last, first = [], []
    for which, k, width in LEVEL_HALO:
        last += [(which, k, rows - width + i) for i in range(width)]
        first += [(which, k, i) for i in range(width)]
    to_down = jnp.concatenate([forcing[:, rows - REACH :].reshape(-1, cols, lanes), jnp.stack(edge(last, lev))])
    to_up = jnp.concatenate([forcing[:, :REACH].reshape(-1, cols, lanes), jnp.stack(edge(first, lev))])
    up = shift(to_down, "gx", 1)
    down = shift(to_up, "gx", -1)

    strips, corners = y_index(reps)
    extra = -(-len(corners) // 16) * 16
    length = len(strips) * rows + extra
    payload = jax.ShapeDtypeStruct((length, lanes), BF16)
    to_left, to_right = pl.pallas_call(
        functools.partial(pack_kernel, reps, rows, cols),
        out_shape=(payload, payload),
        scratch_shapes=[pltpu.VMEM((rows * 8, lanes), F32), pltpu.VMEM((extra, lanes), F32)],
        compiler_params=pltpu.CompilerParams(vmem_limit_bytes=8 * 2**20),
        name="pack",
    )(forcing, lev, up, down)
    right = shift(to_left, "gy", -1)
    left = shift(to_right, "gy", 1)

    vm = pl.BlockSpec(memory_space=pltpu.VMEM)
    size = (rows + 2 * REACH + 2) * WIDE
    adjoints, weighted = pl.pallas_call(
        functools.partial(steps_kernel, reps, rows, cols),
        out_shape=(
            jax.ShapeDtypeStruct((reps, rows, cols, lanes), F32),
            jax.ShapeDtypeStruct((rows, cols, lanes), F32),
        ),
        in_specs=[pl.BlockSpec(memory_space=pltpu.SMEM)] + [vm] * 6,
        out_specs=(hbm, vm),
        scratch_shapes=[pltpu.VMEM((2, reps, size, lanes), F32)]
        + [pltpu.VMEM((size, lanes), F32)] * 4
        + [pltpu.VMEM((2 * extra, lanes), F32), pltpu.VMEM((reps, rows, cols, lanes), F32), pltpu.SemaphoreType.DMA((4,))],
        compiler_params=pltpu.CompilerParams(vmem_limit_bytes=24 * 2**20),
        name="steps",
    )(coefficients, forcing, lev, up, down, left, right)

    parts = lax.all_to_all(weighted.reshape(groups, own, cols, lanes), "rep", 0, 0, tiled=True)
    return jnp.sum(parts, axis=0), adjoints


def solution(mesh):
    placed = (
        P("rep", "gx", "gy", None),
        P("rep", "gx", "gy", None),
        P("rep", "gx", "gy", None),
        P("rep"),
        P("gx", "gy"),
        P(),
    )
    return jax.shard_map(
        local,
        mesh=mesh,
        in_specs=placed,
        out_specs=(P(("gx", "rep"), "gy", None), P("rep", "gx", "gy", None)),
        check_vma=False,
    )
```

```python
import functools

import jax
import jax.numpy as jnp
from jax import lax
from jax.experimental import pallas as pl
from jax.experimental.pallas import tpu as pltpu
from jax.sharding import PartitionSpec as P

F32 = jnp.float32
BF16 = jnp.bfloat16
STEPS = 3
REACH = 3
WIDE = 40
SCALE = 2.0**15
DT = 0.1

LEVEL_HALO = ((0, 0, 3), (1, 0, 2), (0, 1, 2), (1, 1, 1), (0, 2, 1))


def x_index(reps):
    table, at = {}, 0
    for r in range(reps):
        table["f", r] = (at, REACH)
        at += REACH
    for which, level, width in LEVEL_HALO:
        table[which, level] = (at, width)
        at += width
    return table, at


def y_index(reps):
    keys = [("f", r) for r in range(reps)] + [(w, k) for w, k, _ in LEVEL_HALO]
    width = {("f", r): REACH for r in range(reps)}
    width.update({(w, k): n for w, k, n in LEVEL_HALO})
    strips = [(key, d) for key in keys for d in range(1, width[key] + 1)]
    corners = [
        (key, d, e, side)
        for key in keys
        for d in range(1, width[key])
        for e in range(1, width[key] - d + 1)
        for side in (0, 1)
    ]
    return strips, corners


def pack_kernel(reps, rows, cols, f_ref, lev_ref, up_ref, down_ref, left_ref, right_ref, tile, out):
    xi, _ = x_index(reps)
    strips, corners = y_index(reps)
    keys = []
    for key, _ in strips:
        if key not in keys:
            keys.append(key)
    base = len(strips) * rows
    for side, target in ((0, left_ref), (1, right_ref)):
        lo = 0 if side == 0 else cols - 8
        for key in keys:
            for x in range(rows):
                if key[0] == "f":
                    v = f_ref[key[1], x, lo : lo + 8, :]
                else:
                    v = lev_ref[x // 2, key[1], 2 * key[0] + x % 2, lo : lo + 8, :]
                tile[pl.ds(x * 8, 8), :] = v.astype(F32)
            for n, (k, d) in enumerate(strips):
                if k == key:
                    c = d - 1 if side == 0 else 8 - d
                    target[pl.ds(n * rows, rows), :] = tile[pl.ds(c, rows, stride=8), :].astype(target.dtype)
        out[...] = jnp.zeros_like(out)
        for n, (key, d, e, edge) in enumerate(corners):
            first, width = xi[key]
            row = up_ref[first + width - e, lo : lo + 8, :] if edge == 0 else down_ref[first + e - 1, lo : lo + 8, :]
            c = d - 1 if side == 0 else 8 - d
            out[pl.ds(n, 1), :] = row.astype(F32)[c : c + 1]
        target[pl.ds(base, out.shape[0]), :] = out[...].astype(target.dtype)


def own_kernel(groups, own, v_hbm, t_hbm, mask_hbm, out, v_ref, t_ref, mask_ref, sems):
    copies = [
        pltpu.make_async_copy(source, target, sems.at[n])
        for n, (source, target) in enumerate(((mask_hbm, mask_ref), (v_hbm, v_ref), (t_hbm, t_ref)))
    ]
    for copy in copies:
        copy.start()
    copies[0].wait()
    ocean = jnp.transpose(mask_ref[...].astype(F32))
    copies[1].wait()
    for x in range(groups * own):
        out[x // own, x % own] = v_ref[0, x] * BF16(SCALE)
    copies[2].wait()
    for x in range(groups * own):
        t = t_ref[0, x].astype(F32)
        out[x // own, own + x % own] = jnp.where(ocean[:, x : x + 1] > 0.0, t, 0.0).astype(BF16)


def pick_kernel(levels_ref, slices_ref, out):
    for k in range(STEPS):
        out[k] = slices_ref[levels_ref[k]]


def sweep(body, start, count, by=8):
    def several(g, carry):
        for i in range(by):
            body(start + g * by + i, carry)
        return carry

    lax.fori_loop(0, count // by, several, 0)
    for i in range(count // by * by, count):
        body(start + i, 0)


def steps_kernel(
    reps, rows, cols,
    coef_ref, f_ref, lev_ref, up_ref, down_ref, left_ref, right_ref,
    adj_hbm, sum_ref,
    state, vx, vy, keep, swap, spare, adj_ref, sems,
):
    xi, _ = x_index(reps)
    strips, corners = y_index(reps)
    total = rows + 2 * REACH
    base = len(strips) * rows
    half = 64
    extra = spare.shape[0] // 2

    def put_state(r):
        def put(at, v):
            state[0, r, at, :] = v

        return put

    def put_speed(at, v):
        v = v * (0.5 * DT / SCALE)
        o = pltpu.roll(v, half, axis=1)
        is_low = lax.broadcasted_iota(jnp.int32, v.shape, 1) < half
        vx[at, :] = jnp.where(is_low, v, o)
        vy[at, :] = jnp.where(is_low, o, v)

    def put_tracer(at, t):
        keep[at, :] = jnp.where(t > 0.0, (1.0 - 4.0 * DT) - DT * t, 4.0)
        swap[at, :] = DT * pltpu.roll(t, half, axis=1)

    def fill(put, key):
        if key in xi:
            first, width = xi[key]
            for e in range(1, width + 1):
                put(pl.ds((REACH - e + 1) * WIDE, cols), up_ref[first + width - e].astype(F32))
                put(pl.ds((REACH + rows + e) * WIDE, cols), down_ref[first + e - 1].astype(F32))
        for side, source in ((0, left_ref), (1, right_ref)):
            for n, (k, d) in enumerate(strips):
                if k == key:
                    c = -d if side == 0 else cols + d - 1
                    at = pl.ds((REACH + 1) * WIDE + c, rows, stride=WIDE)
                    put(at, source[pl.ds(n * rows, rows), :].astype(F32))
            for n, (k, d, e, edge) in enumerate(corners):
                if k == key:
                    c = -d if side == 0 else cols + d - 1
                    x = REACH - e if edge == 0 else REACH + rows + e - 1
                    put(pl.ds((x + 1) * WIDE + c, 1), spare[pl.ds(side * extra + n, 1), :])

    spare[pl.ds(0, extra), :] = left_ref[pl.ds(base, extra), :].astype(F32)
    spare[pl.ds(extra, extra), :] = right_ref[pl.ds(base, extra), :].astype(F32)

    def forcing_row(x, carry):
        at = pl.ds(pl.multiple_of((x + REACH + 1) * WIDE, 8), cols)
        for r in range(reps):
            state[0, r, at, :] = f_ref[r, x].astype(F32)
        return carry

    lax.fori_loop(0, rows, forcing_row, 0, unroll=4)
    for r in range(reps):
        fill(put_state(r), ("f", r))

    for k in range(STEPS):
        now, later = k % 2, (k + 1) % 2

        def level_rows(g, carry, k=k):
            own = lev_ref.shape[2] // 2
            for i in range(own):
                at = pl.ds(pl.multiple_of((g * own + i + REACH + 1) * WIDE, 8), cols)
                put_speed(at, lev_ref[g, k, i].astype(F32))
                put_tracer(at, lev_ref[g, k, own + i].astype(F32))
            return carry

        lax.fori_loop(0, lev_ref.shape[0], level_rows, 0, unroll=4)
        fill(put_speed, (0, k))
        fill(put_tracer, (1, k))

        def row(x, carry, k=k, now=now, later=later):
            start = pl.multiple_of(x * WIDE, 8)
            for j in range(0, cols if k == STEPS - 1 else WIDE, 8):
                at = pl.ds(start + j, 8)
                above, below = pl.ds(start + j - WIDE, 8), pl.ds(start + j + WIDE, 8)
                before, after = pl.ds(start + j - 1, 8), pl.ds(start + j + 1, 8)
                a = DT + vx[above, :]
                b = DT - vx[below, :]
                c = DT + vy[before, :]
                d = DT - vy[after, :]
                centre = keep[at, :]
                other = swap[at, :]
                ocean = centre < 1.0
                weighted = None
                for r in range(reps):
                    s = state[now, r, at, :]
                    new = (
                        (a * state[now, r, above, :] + b * state[now, r, below, :])
                        + (c * state[now, r, before, :] + d * state[now, r, after, :])
                        + (centre * s + other * pltpu.roll(s, half, axis=1))
                    )
                    new = jnp.where(ocean, new, 0.0)
                    if k < STEPS - 1:
                        state[later, r, at, :] = new
                    else:
                        adj_ref[r, x - REACH - 1, pl.ds(j, 8)] = new
                        part = coef_ref[r] * new
                        weighted = part if weighted is None else weighted + part
                if k == STEPS - 1:
                    sum_ref[x - REACH - 1, pl.ds(j, 8)] = weighted
            return carry

        if k < STEPS - 1:
            sweep(row, k + 1, total - 2 * k - 1)

    stretch = rows // sems.shape[0]

    def out_copy(g):
        at = pl.ds(g * stretch, stretch)
        return pltpu.make_async_copy(adj_ref.at[:, at], adj_hbm.at[:, at], sems.at[g])

    def some_rows(g, carry):
        sweep(row, REACH + 1 + g * stretch, stretch)
        out_copy(g).start()
        return carry

    lax.fori_loop(0, sems.shape[0], some_rows, 0)
    for g in range(sems.shape[0]):
        out_copy(g).wait()


def shift(x, axis, by):
    n = lax.axis_size(axis)
    if by > 0:
        return lax.ppermute(x, axis, [(i, i + 1) for i in range(n - 1)])
    return lax.ppermute(x, axis, [(i + 1, i) for i in range(n - 1)])


def local(velocity, tracers, forcing, coefficients, land_mask, step_levels):
    groups = lax.axis_size("rep")
    reps, rows, cols, lanes = forcing.shape
    own = rows // groups
    hbm = pl.BlockSpec(memory_space=pltpu.HBM)
    mine = pl.pallas_call(
        functools.partial(own_kernel, groups, own),
        out_shape=jax.ShapeDtypeStruct((groups, 2 * own, cols, lanes), BF16),
        in_specs=[hbm] * 3,
        scratch_shapes=[
            pltpu.VMEM(velocity.shape, BF16),
            pltpu.VMEM(tracers.shape, BF16),
            pltpu.VMEM(land_mask.shape, land_mask.dtype),
            pltpu.SemaphoreType.DMA((3,)),
        ],
        compiler_params=pltpu.CompilerParams(vmem_limit_bytes=8 * 2**20),
        name="own",
    )(*(pltpu.with_memory_space_constraint(x, pltpu.HBM) for x in (velocity, tracers, land_mask)))
    slices = lax.all_to_all(mine, "rep", 0, 0, tiled=True)
    slices, forcing, step_levels = lax.optimization_barrier((slices, forcing, step_levels))
    picked = pl.pallas_call(
        pick_kernel,
        out_shape=jax.ShapeDtypeStruct((STEPS, 2 * own, cols, lanes), BF16),
        in_specs=[pl.BlockSpec(memory_space=pltpu.SMEM), pl.BlockSpec(memory_space=pltpu.VMEM)],
        compiler_params=pltpu.CompilerParams(vmem_limit_bytes=8 * 2**20),
        name="pick",
    )(step_levels, slices)
    lev = lax.all_gather(picked.astype(jnp.float16), "rep", axis=0, tiled=False)
    lev = lax.optimization_barrier(lev).astype(BF16)

    def edge(rows_of, source):
        return [source[x // own, k, which * own + x % own] for which, k, x in rows_of]

    last, first = [], []
    for which, k, width in LEVEL_HALO:
        last += [(which, k, rows - width + i) for i in range(width)]
        first += [(which, k, i) for i in range(width)]
    to_down = jnp.concatenate([forcing[:, rows - REACH :].reshape(-1, cols, lanes), jnp.stack(edge(last, lev))])
    to_up = jnp.concatenate([forcing[:, :REACH].reshape(-1, cols, lanes), jnp.stack(edge(first, lev))])
    up = shift(to_down, "gx", 1)
    down = shift(to_up, "gx", -1)

    strips, corners = y_index(reps)
    extra = -(-len(corners) // 16) * 16
    length = len(strips) * rows + extra
    payload = jax.ShapeDtypeStruct((length, lanes), BF16)
    to_left, to_right = pl.pallas_call(
        functools.partial(pack_kernel, reps, rows, cols),
        out_shape=(payload, payload),
        scratch_shapes=[pltpu.VMEM((rows * 8, lanes), F32), pltpu.VMEM((extra, lanes), F32)],
        compiler_params=pltpu.CompilerParams(vmem_limit_bytes=8 * 2**20),
        name="pack",
    )(forcing, lev, up, down)
    right = shift(to_left, "gy", -1)
    left = shift(to_right, "gy", 1)

    vm = pl.BlockSpec(memory_space=pltpu.VMEM)
    size = (rows + 2 * REACH + 2) * WIDE
    adjoints, weighted = pl.pallas_call(
        functools.partial(steps_kernel, reps, rows, cols),
        out_shape=(
            jax.ShapeDtypeStruct((reps, rows, cols, lanes), F32),
            jax.ShapeDtypeStruct((rows, cols, lanes), F32),
        ),
        in_specs=[pl.BlockSpec(memory_space=pltpu.SMEM)] + [vm] * 6,
        out_specs=(hbm, vm),
        scratch_shapes=[pltpu.VMEM((2, reps, size, lanes), F32)]
        + [pltpu.VMEM((size, lanes), F32)] * 4
        + [pltpu.VMEM((2 * extra, lanes), F32), pltpu.VMEM((reps, rows, cols, lanes), F32), pltpu.SemaphoreType.DMA((4,))],
        compiler_params=pltpu.CompilerParams(vmem_limit_bytes=24 * 2**20),
        name="steps",
    )(coefficients, forcing, lev, up, down, left, right)

    parts = lax.all_to_all(weighted.reshape(groups, own, cols, lanes), "rep", 0, 0, tiled=True)
    return jnp.sum(parts, axis=0), adjoints


def solution(mesh):
    placed = (
        P("rep", "gx", "gy", None),
        P("rep", "gx", "gy", None),
        P("rep", "gx", "gy", None),
        P("rep"),
        P("gx", "gy"),
        P(),
    )
    return jax.shard_map(
        local,
        mesh=mesh,
        in_specs=placed,
        out_specs=(P(("gx", "rep"), "gy", None), P("rep", "gx", "gy", None)),
        check_vma=False,
    )
```

```python
import functools

import jax
import jax.numpy as jnp
from jax import lax
from jax.experimental import pallas as pl
from jax.experimental.pallas import tpu as pltpu
from jax.sharding import PartitionSpec as P

F32 = jnp.float32
BF16 = jnp.bfloat16
STEPS = 3
REACH = 3
SCALE = 2.0**15
DT = 0.1
HALF = 64
LAND = 4.0
TALL = 38
DEEP = 6

LEVEL_HALO = ((0, 0, 3), (1, 0, 2), (0, 1, 2), (1, 1, 1), (0, 2, 1))


def x_index(reps):
    table, at = {}, 0
    for r in range(reps):
        table["f", r] = (at, REACH)
        at += REACH
    for which, level, width in LEVEL_HALO:
        table[which, level] = (at, width)
        at += width
    return table, at


def y_index(reps):
    keys = [("f", r) for r in range(reps)] + [(w, k) for w, k, _ in LEVEL_HALO]
    width = {("f", r): REACH for r in range(reps)}
    width.update({(w, k): n for w, k, n in LEVEL_HALO})
    strips = [(key, d) for key in keys for d in range(1, width[key] + 1)]
    corners = [
        (key, d, e, side)
        for key in keys
        for d in range(1, width[key])
        for e in range(1, width[key] - d + 1)
        for side in (0, 1)
    ]
    return strips, corners


def pack_kernel(reps, rows, cols, f_ref, lev_ref, up_ref, down_ref, left_ref, right_ref, tile, out):
    xi, _ = x_index(reps)
    strips, corners = y_index(reps)
    keys = []
    for key, _ in strips:
        if key not in keys:
            keys.append(key)
    base = len(strips) * rows
    for side, target in ((0, left_ref), (1, right_ref)):
        lo = 0 if side == 0 else cols - 8
        for key in keys:
            for x in range(rows):
                if key[0] == "f":
                    v = f_ref[key[1], x, lo : lo + 8, :]
                else:
                    v = lev_ref[x // 2, key[1], 2 * key[0] + x % 2, lo : lo + 8, :]
                tile[pl.ds(x * 8, 8), :] = v.astype(F32)
            for n, (k, d) in enumerate(strips):
                if k == key:
                    c = d - 1 if side == 0 else 8 - d
                    target[pl.ds(n * rows, rows), :] = tile[pl.ds(c, rows, stride=8), :].astype(target.dtype)
        out[...] = jnp.zeros_like(out)
        for n, (key, d, e, edge) in enumerate(corners):
            first, width = xi[key]
            row = up_ref[first + width - e, lo : lo + 8, :] if edge == 0 else down_ref[first + e - 1, lo : lo + 8, :]
            c = d - 1 if side == 0 else 8 - d
            out[pl.ds(n, 1), :] = row.astype(F32)[c : c + 1]
        target[pl.ds(base, out.shape[0]), :] = out[...].astype(target.dtype)


def own_kernel(groups, own, v_hbm, t_hbm, mask_hbm, out, v_ref, t_ref, mask_ref, sems):
    copies = [
        pltpu.make_async_copy(source, target, sems.at[n])
        for n, (source, target) in enumerate(((mask_hbm, mask_ref), (v_hbm, v_ref), (t_hbm, t_ref)))
    ]
    for copy in copies:
        copy.start()
    copies[0].wait()
    ocean = jnp.transpose(mask_ref[...].astype(F32))
    copies[1].wait()
    for x in range(groups * own):
        out[x // own, x % own] = v_ref[0, x] * BF16(SCALE)
    copies[2].wait()
    for x in range(groups * own):
        t = t_ref[0, x].astype(F32)
        out[x // own, own + x % own] = jnp.where(ocean[:, x : x + 1] > 0.0, t, 0.0).astype(BF16)


def pick_kernel(levels_ref, slices_ref, out):
    for k in range(STEPS):
        out[k] = slices_ref[levels_ref[k]]


def combine(coef_ref, news):
    total = None
    for r, new in enumerate(news):
        part = coef_ref[r] * new
        total = part if total is None else total + part
    return total


def speed_terms(v):
    v = v * (0.5 * DT / SCALE)
    o = pltpu.roll(v, HALF, axis=1)
    low = lax.broadcasted_iota(jnp.int32, v.shape, 1) < HALF
    return jnp.where(low, v, o), jnp.where(low, o, v)


def tracer_terms(t):
    return jnp.where(t > 0.0, (1.0 - 4.0 * DT) - DT * t, LAND), DT * pltpu.roll(t, HALF, axis=1)


def edge_columns(k):
    return (5 - k, 6 - k, 5 - k, 5 - k)


def sweep(body, start, count, by=8):
    def several(g, carry):
        for i in range(by):
            body(start + g * by + i, carry)
        return carry

    lax.fori_loop(0, count // by, several, 0)
    for i in range(count // by * by, count):
        body(start + i, 0)


def inner_kernel(
    reps, rows, cols,
    coef_ref, f_ref, lev_ref, up_ref, down_ref,
    adj_hbm, sum_ref, edge_state, edge_terms, tiles,
    state, vx, vy, keep, swap, adj_ref, sems,
):
    xi, _ = x_index(reps)
    total = rows + 2 * REACH
    own = lev_ref.shape[2] // 2

    def slot(x):
        return pl.ds(pl.multiple_of((x + 1) * cols, 8), cols)

    def put_speed(x, v):
        vx[slot(x), :], vy[slot(x), :] = speed_terms(v)

    def put_tracer(x, t):
        keep[slot(x), :], swap[slot(x), :] = tracer_terms(t)

    def put_rows(put, key):
        if key in xi:
            first, width = xi[key]
            for e in range(1, width + 1):
                put(REACH - e, up_ref[first + width - e].astype(F32))
                put(REACH + rows + e - 1, down_ref[first + e - 1].astype(F32))

    def forcing_row(x, carry):
        for r in range(reps):
            state[0, r, slot(x + REACH), :] = f_ref[r, x].astype(F32)
        return carry

    lax.fori_loop(0, rows, forcing_row, 0, unroll=4)
    for r in range(reps):

        def put_state(x, v, r=r):
            state[0, r, slot(x), :] = v

        put_rows(put_state, ("f", r))
        for side in (0, 1):
            for depth in range(edge_state.shape[2]):
                y = depth if side == 0 else cols - 1 - depth
                edge_state[side, r, depth] = state[0, r, pl.ds(cols + y, TALL, stride=cols), :]

    for k in range(STEPS):
        now, later = k % 2, (k + 1) % 2

        def level_rows(g, carry, k=k):
            for i in range(own):
                put_speed(g * own + i + REACH, lev_ref[g, k, i].astype(F32))
                put_tracer(g * own + i + REACH, lev_ref[g, k, own + i].astype(F32))
            return carry

        lax.fori_loop(0, lev_ref.shape[0], level_rows, 0, unroll=4)
        put_rows(put_speed, (0, k))
        put_rows(put_tracer, (1, k))
        for side in (0, 1):
            for n, (source, count) in enumerate(zip((vx, vy, keep, swap), edge_columns(k))):
                for depth in range(count):
                    y = depth if side == 0 else cols - 1 - depth
                    edge_terms[side, k, n, depth] = source[pl.ds(cols + y, TALL, stride=cols), :]

        def row(x, carry, k=k, now=now, later=later):
            start = pl.multiple_of((x + 1) * cols, 8)
            for j in range(0, cols, 8):
                at = pl.ds(start + j, 8)
                above, below = pl.ds(start + j - cols, 8), pl.ds(start + j + cols, 8)
                before, after = pl.ds(start + j - 1, 8), pl.ds(start + j + 1, 8)
                a = DT + vx[above, :]
                b = DT - vx[below, :]
                c = DT + vy[before, :]
                d = DT - vy[after, :]
                centre = keep[at, :]
                other = swap[at, :]
                ocean = centre < 1.0
                news = []
                for r in range(reps):
                    s = state[now, r, at, :]
                    new = (
                        (a * state[now, r, above, :] + b * state[now, r, below, :])
                        + (c * state[now, r, before, :] + d * state[now, r, after, :])
                        + (centre * s + other * pltpu.roll(s, HALF, axis=1))
                    )
                    new = jnp.where(ocean, new, 0.0)
                    if k < STEPS - 1:
                        state[later, r, at, :] = new
                    else:
                        adj_ref[r, pl.ds(pl.multiple_of((x - REACH) * cols, 8) + j, 8), :] = new
                        if j in (0, cols - 8):
                            tiles[min(j, 1), r, pl.ds(pl.multiple_of((x - REACH) * 8, 8), 8), :] = new
                        news.append(new)
                if news:
                    sum_ref[pl.ds(pl.multiple_of((x - REACH) * cols, 8) + j, 8), :] = combine(coef_ref, news)
            return carry

        if k < STEPS - 1:
            sweep(row, k + 1, total - 2 * k - 2)

    stretch = rows // sems.shape[0]

    def out_copy(g):
        at = pl.ds(g * stretch * cols, stretch * cols)
        return pltpu.make_async_copy(adj_ref.at[:, at], adj_hbm.at[:, at], sems.at[g])

    def some_rows(g, carry):
        sweep(row, REACH + g * stretch, stretch)
        out_copy(g).start()
        return carry

    lax.fori_loop(0, sems.shape[0], some_rows, 0)
    for g in range(sems.shape[0]):
        out_copy(g).wait()


def edge_kernel(
    reps, rows, cols,
    coef_ref, edge_state, edge_terms, left_ref, right_ref, tiles_in, adj_in, sum_in,
    tiles, adj_hbm, sum_ref,
    halo_state, halo_terms, state, spare, sems,
):
    del tiles_in, adj_in, sum_in
    strips, corners = y_index(reps)
    base = len(strips) * rows
    extra = spare.shape[0]

    def out_copy(side):
        target = adj_hbm.at[:, :, pl.ds(side * (cols - 8), 8)]
        return pltpu.make_async_copy(tiles.at[side].reshape(reps, rows, 8, 128), target, sems.at[side])

    for side, source in ((0, left_ref), (1, right_ref)):
        spare[...] = source[pl.ds(base, extra), :].astype(F32)

        def put(key, q, at, v, side=side):
            if key[0] == "f":
                halo_state[side, key[1], q, at, :] = v
            elif key[0] == 0:
                halo_terms[side, key[1], 0, q, at, :], halo_terms[side, key[1], 1, q, at, :] = speed_terms(v)
            else:
                halo_terms[side, key[1], 2, q, at, :], halo_terms[side, key[1], 3, q, at, :] = tracer_terms(v)

        for n, (key, d) in enumerate(strips):
            put(key, REACH - d, pl.ds(8 + REACH, rows), source[pl.ds(n * rows, rows), :].astype(F32))
        for n, (key, d, e, edge) in enumerate(corners):
            x = REACH - e if edge == 0 else REACH + rows + e - 1
            put(key, REACH - d, pl.ds(8 + x, 1), spare[pl.ds(n, 1), :])

        sign = 1.0 if side == 0 else -1.0

        def term(k, n, q, start, size, side=side):
            if q < REACH:
                return halo_terms[side, k, n, q, pl.ds(8 + start, size), :]
            return edge_terms[side, k, n, q - REACH, pl.ds(start, size), :]

        def cell(k, r, q, start, size, side=side):
            if k > 0:
                return state[(k - 1) % 2, r, q, pl.ds(8 + start, size), :]
            if q < REACH:
                return halo_state[side, r, q, pl.ds(8 + start, size), :]
            return edge_state[side, r, q - REACH, pl.ds(start, size), :]

        for k in range(STEPS):
            for q in range(k + 1, 8 - k):
                for start in range(k + 1, k + 1 + rows + 2 * (REACH - k - 1), 8):
                    size = min(8, k + 1 + rows + 2 * (REACH - k - 1) - start)
                    a = DT + term(k, 0, q, start - 1, size)
                    b = DT - term(k, 0, q, start + 1, size)
                    c = DT + sign * term(k, 1, q - 1, start, size)
                    d = DT - sign * term(k, 1, q + 1, start, size)
                    centre = term(k, 2, q, start, size)
                    other = term(k, 3, q, start, size)
                    ocean = centre < 1.0
                    news = []
                    for r in range(reps):
                        s = cell(k, r, q, start, size)
                        new = (
                            (a * cell(k, r, q, start - 1, size) + b * cell(k, r, q, start + 1, size))
                            + (c * cell(k, r, q - 1, start, size) + d * cell(k, r, q + 1, start, size))
                            + (centre * s + other * pltpu.roll(s, HALF, axis=1))
                        )
                        new = jnp.where(ocean, new, 0.0)
                        if k < STEPS - 1:
                            state[k % 2, r, q, pl.ds(8 + start, size), :] = new
                        news.append(new)
                    if k == STEPS - 1:
                        y = q - REACH if side == 0 else cols - 1 - (q - REACH)
                        sum_ref[pl.ds((start - REACH) * cols + y, size, stride=cols), :] = combine(coef_ref, news)
                        y = q - REACH if side == 0 else 7 - (q - REACH)
                        for r in range(reps):
                            tiles[side, r, pl.ds((start - REACH) * 8 + y, size, stride=8), :] = news[r]
        out_copy(side).start()
    for side in (0, 1):
        out_copy(side).wait()


def shift(x, axis, by):
    n = lax.axis_size(axis)
    if by > 0:
        return lax.ppermute(x, axis, [(i, i + 1) for i in range(n - 1)])
    return lax.ppermute(x, axis, [(i + 1, i) for i in range(n - 1)])


def local(velocity, tracers, forcing, coefficients, land_mask, step_levels):
    groups = lax.axis_size("rep")
    reps, rows, cols, lanes = forcing.shape
    own = rows // groups
    hbm = pl.BlockSpec(memory_space=pltpu.HBM)
    mine = pl.pallas_call(
        functools.partial(own_kernel, groups, own),
        out_shape=jax.ShapeDtypeStruct((groups, 2 * own, cols, lanes), BF16),
        in_specs=[hbm] * 3,
        scratch_shapes=[
            pltpu.VMEM(velocity.shape, BF16),
            pltpu.VMEM(tracers.shape, BF16),
            pltpu.VMEM(land_mask.shape, land_mask.dtype),
            pltpu.SemaphoreType.DMA((3,)),
        ],
        compiler_params=pltpu.CompilerParams(vmem_limit_bytes=8 * 2**20),
        name="own",
    )(*(pltpu.with_memory_space_constraint(x, pltpu.HBM) for x in (velocity, tracers, land_mask)))
    slices = lax.all_to_all(mine, "rep", 0, 0, tiled=True)
    slices, forcing, step_levels = lax.optimization_barrier((slices, forcing, step_levels))
    picked = pl.pallas_call(
        pick_kernel,
        out_shape=jax.ShapeDtypeStruct((STEPS, 2 * own, cols, lanes), BF16),
        in_specs=[pl.BlockSpec(memory_space=pltpu.SMEM), pl.BlockSpec(memory_space=pltpu.VMEM)],
        compiler_params=pltpu.CompilerParams(vmem_limit_bytes=8 * 2**20),
        name="pick",
    )(step_levels, slices)
    lev = lax.all_gather(picked.astype(jnp.float16), "rep", axis=0, tiled=False)
    lev = lax.optimization_barrier(lev).astype(BF16)

    def edge(rows_of, source):
        return [source[x // own, k, which * own + x % own] for which, k, x in rows_of]

    last, first = [], []
    for which, k, width in LEVEL_HALO:
        last += [(which, k, rows - width + i) for i in range(width)]
        first += [(which, k, i) for i in range(width)]
    to_down = jnp.concatenate([forcing[:, rows - REACH :].reshape(-1, cols, lanes), jnp.stack(edge(last, lev))])
    to_up = jnp.concatenate([forcing[:, :REACH].reshape(-1, cols, lanes), jnp.stack(edge(first, lev))])
    up = shift(to_down, "gx", 1)
    down = shift(to_up, "gx", -1)

    strips, corners = y_index(reps)
    extra = -(-len(corners) // 16) * 16
    length = len(strips) * rows + extra
    payload = jax.ShapeDtypeStruct((length, lanes), BF16)
    to_left, to_right = pl.pallas_call(
        functools.partial(pack_kernel, reps, rows, cols),
        out_shape=(payload, payload),
        scratch_shapes=[pltpu.VMEM((rows * 8, lanes), F32), pltpu.VMEM((extra, lanes), F32)],
        compiler_params=pltpu.CompilerParams(vmem_limit_bytes=8 * 2**20),
        name="pack",
    )(forcing, lev, up, down)
    right = shift(to_left, "gy", -1)
    left = shift(to_right, "gy", 1)

    vm = pl.BlockSpec(memory_space=pltpu.VMEM)
    sm = pl.BlockSpec(memory_space=pltpu.SMEM)
    size = (rows + 2 * REACH + 2) * cols
    total = jax.ShapeDtypeStruct((rows * cols, lanes), F32)
    tiled = jax.ShapeDtypeStruct((2, reps, rows * 8, lanes), F32)
    adjoints, weighted, edge_state, edge_terms, tiles = pl.pallas_call(
        functools.partial(inner_kernel, reps, rows, cols),
        out_shape=(
            jax.ShapeDtypeStruct((reps, rows * cols, lanes), F32),
            total,
            jax.ShapeDtypeStruct((2, reps, DEEP, TALL, lanes), F32),
            jax.ShapeDtypeStruct((2, STEPS, 4, DEEP, TALL, lanes), F32),
            tiled,
        ),
        in_specs=[sm] + [vm] * 4,
        out_specs=(hbm,) + (vm,) * 4,
        scratch_shapes=[pltpu.VMEM((2, reps, size, lanes), F32)]
        + [pltpu.VMEM((size, lanes), F32)] * 4
        + [pltpu.VMEM((reps, rows * cols, lanes), F32), pltpu.SemaphoreType.DMA((4,))],
        compiler_params=pltpu.CompilerParams(vmem_limit_bytes=24 * 2**20),
        name="inner",
    )(coefficients, forcing, lev, up, down)
    adjoints = adjoints.reshape(reps, rows, cols, lanes)
    long = 8 + TALL + 2
    _, adjoints, weighted = pl.pallas_call(
        functools.partial(edge_kernel, reps, rows, cols),
        out_shape=(tiled, jax.ShapeDtypeStruct(adjoints.shape, F32), total),
        in_specs=[sm] + [vm] * 5 + [hbm, vm],
        out_specs=(vm, hbm, vm),
        scratch_shapes=[
            pltpu.VMEM((2, reps, REACH, long, lanes), F32),
            pltpu.VMEM((2, STEPS, 4, REACH, long, lanes), F32),
            pltpu.VMEM((2, reps, REACH + DEEP, long, lanes), F32),
            pltpu.VMEM((extra, lanes), F32),
            pltpu.SemaphoreType.DMA((2,)),
        ],
        input_output_aliases={5: 0, 6: 1, 7: 2},
        compiler_params=pltpu.CompilerParams(vmem_limit_bytes=12 * 2**20),
        name="edge",
    )(coefficients, edge_state, edge_terms, left, right, tiles, adjoints, weighted)

    parts = lax.all_to_all(weighted.reshape(groups, own, cols, lanes), "rep", 0, 0, tiled=True)
    return jnp.sum(parts, axis=0), adjoints


def solution(mesh):
    placed = (
        P("rep", "gx", "gy", None),
        P("rep", "gx", "gy", None),
        P("rep", "gx", "gy", None),
        P("rep"),
        P("gx", "gy"),
        P(),
    )
    return jax.shard_map(
        local,
        mesh=mesh,
        in_specs=placed,
        out_specs=(P(("gx", "rep"), "gy", None), P("rep", "gx", "gy", None)),
        check_vma=False,
    )
```

```python
import functools

import jax
import jax.numpy as jnp
from jax import lax
from jax.experimental import pallas as pl
from jax.experimental.pallas import tpu as pltpu
from jax.sharding import PartitionSpec as P

F32 = jnp.float32
BF16 = jnp.bfloat16
STEPS = 3
REACH = 3
SCALE = 2.0**15
DT = 0.1
HALF = 64
LAND = 4.0
TALL = 38
DEEP = 6

LEVEL_HALO = ((0, 0, 3), (1, 0, 2), (0, 1, 2), (1, 1, 1), (0, 2, 1))


def x_index(reps):
    table, at = {}, 0
    for r in range(reps):
        table["f", r] = (at, REACH)
        at += REACH
    for which, level, width in LEVEL_HALO:
        table[which, level] = (at, width)
        at += width
    return table, at


def y_index(reps):
    keys = [("f", r) for r in range(reps)] + [(w, k) for w, k, _ in LEVEL_HALO]
    width = {("f", r): REACH for r in range(reps)}
    width.update({(w, k): n for w, k, n in LEVEL_HALO})
    strips = [(key, d) for key in keys for d in range(1, width[key] + 1)]
    corners = [
        (key, d, e, side)
        for key in keys
        for d in range(1, width[key])
        for e in range(1, width[key] - d + 1)
        for side in (0, 1)
    ]
    return strips, corners


def swaps(x, axis, first):
    ends = lax.axis_size(axis) - 1
    return lax.ppermute(x, axis, [p for i in range(first, ends, 2) for p in ((i, i + 1), (i + 1, i))])


def pack_kernel(reps, rows, cols, f_ref, lev_ref, up_ref, down_ref, even_ref, odd_ref, both, tile, out):
    xi, _ = x_index(reps)
    strips, corners = y_index(reps)
    keys = []
    for key, _ in strips:
        if key not in keys:
            keys.append(key)
    base = len(strips) * rows
    for side in (0, 1):
        target = both.at[side]
        lo = 0 if side == 0 else cols - 8
        for key in keys:
            for x in range(rows):
                if key[0] == "f":
                    v = f_ref[key[1], x, lo : lo + 8, :]
                else:
                    v = lev_ref[x // 2, key[1], 2 * key[0] + x % 2, lo : lo + 8, :]
                tile[pl.ds(x * 8, 8), :] = v.astype(F32)
            for n, (k, d) in enumerate(strips):
                if k == key:
                    c = d - 1 if side == 0 else 8 - d
                    target[pl.ds(n * rows, rows), :] = tile[pl.ds(c, rows, stride=8), :].astype(target.dtype)
        out[...] = jnp.zeros_like(out)
        for n, (key, d, e, edge) in enumerate(corners):
            first, width = xi[key]
            row = up_ref[first + width - e, lo : lo + 8, :] if edge == 0 else down_ref[first + e - 1, lo : lo + 8, :]
            c = d - 1 if side == 0 else 8 - d
            out[pl.ds(n, 1), :] = row.astype(F32)[c : c + 1]
        target[pl.ds(base, out.shape[0]), :] = out[...].astype(target.dtype)
    parity = lax.rem(lax.axis_index("gy"), 2)
    even_ref[...] = both[1 - parity]
    odd_ref[...] = both[parity]


def own_kernel(groups, own, v_hbm, t_hbm, mask_hbm, out, v_ref, t_ref, mask_ref, sems):
    copies = [
        pltpu.make_async_copy(source, target, sems.at[n])
        for n, (source, target) in enumerate(((mask_hbm, mask_ref), (v_hbm, v_ref), (t_hbm, t_ref)))
    ]
    for copy in copies:
        copy.start()
    copies[0].wait()
    ocean = jnp.transpose(mask_ref[...].astype(F32))
    copies[1].wait()
    for x in range(groups * own):
        out[x // own, x % own] = v_ref[0, x] * BF16(SCALE)
    copies[2].wait()
    for x in range(groups * own):
        t = t_ref[0, x].astype(F32)
        out[x // own, own + x % own] = jnp.where(ocean[:, x : x + 1] > 0.0, t, 0.0).astype(BF16)


def pick_kernel(levels_ref, slices_ref, out):
    for k in range(STEPS):
        out[k] = slices_ref[levels_ref[k]]


def combine(coef_ref, news):
    total = None
    for r, new in enumerate(news):
        part = coef_ref[r] * new
        total = part if total is None else total + part
    return total


def speed_terms(v):
    v = v * (0.5 * DT / SCALE)
    o = pltpu.roll(v, HALF, axis=1)
    low = lax.broadcasted_iota(jnp.int32, v.shape, 1) < HALF
    return jnp.where(low, v, o), jnp.where(low, o, v)


def tracer_terms(t):
    return jnp.where(t > 0.0, (1.0 - 4.0 * DT) - DT * t, LAND), DT * pltpu.roll(t, HALF, axis=1)


def edge_columns(k):
    return (5 - k, 6 - k, 5 - k, 5 - k)


def sweep(body, start, count, by=8):
    def several(g, carry):
        for i in range(by):
            body(start + g * by + i, carry)
        return carry

    lax.fori_loop(0, count // by, several, 0)
    for i in range(count // by * by, count):
        body(start + i, 0)


def inner_kernel(
    reps, rows, cols,
    coef_ref, f_ref, lev_ref, up_ref, down_ref,
    adj_hbm, sum_ref, edge_state, edge_terms, tiles,
    state, vx, vy, keep, swap, adj_ref, sems,
):
    xi, _ = x_index(reps)
    total = rows + 2 * REACH
    own = lev_ref.shape[2] // 2

    def slot(x):
        return pl.ds(pl.multiple_of((x + 1) * cols, 8), cols)

    def put_speed(x, v):
        vx[slot(x), :], vy[slot(x), :] = speed_terms(v)

    def put_tracer(x, t):
        keep[slot(x), :], swap[slot(x), :] = tracer_terms(t)

    def put_rows(put, key):
        if key in xi:
            first, width = xi[key]
            for e in range(1, width + 1):
                put(REACH - e, up_ref[first + width - e].astype(F32))
                put(REACH + rows + e - 1, down_ref[first + e - 1].astype(F32))

    def forcing_row(x, carry):
        for r in range(reps):
            state[0, r, slot(x + REACH), :] = f_ref[r, x].astype(F32)
        return carry

    lax.fori_loop(0, rows, forcing_row, 0, unroll=4)
    for r in range(reps):

        def put_state(x, v, r=r):
            state[0, r, slot(x), :] = v

        put_rows(put_state, ("f", r))
        for side in (0, 1):
            for depth in range(edge_state.shape[2]):
                y = depth if side == 0 else cols - 1 - depth
                edge_state[side, r, depth] = state[0, r, pl.ds(cols + y, TALL, stride=cols), :]

    for k in range(STEPS):
        now, later = k % 2, (k + 1) % 2

        def level_rows(g, carry, k=k):
            for i in range(own):
                put_speed(g * own + i + REACH, lev_ref[g, k, i].astype(F32))
                put_tracer(g * own + i + REACH, lev_ref[g, k, own + i].astype(F32))
            return carry

        lax.fori_loop(0, lev_ref.shape[0], level_rows, 0, unroll=4)
        put_rows(put_speed, (0, k))
        put_rows(put_tracer, (1, k))
        for side in (0, 1):
            for n, (source, count) in enumerate(zip((vx, vy, keep, swap), edge_columns(k))):
                for depth in range(count):
                    y = depth if side == 0 else cols - 1 - depth
                    edge_terms[side, k, n, depth] = source[pl.ds(cols + y, TALL, stride=cols), :]

        def row(x, carry, k=k, now=now, later=later):
            start = pl.multiple_of((x + 1) * cols, 8)
            for j in range(0, cols, 8):
                at = pl.ds(start + j, 8)
                above, below = pl.ds(start + j - cols, 8), pl.ds(start + j + cols, 8)
                before, after = pl.ds(start + j - 1, 8), pl.ds(start + j + 1, 8)
                a = DT + vx[above, :]
                b = DT - vx[below, :]
                c = DT + vy[before, :]
                d = DT - vy[after, :]
                centre = keep[at, :]
                other = swap[at, :]
                ocean = centre < 1.0
                news = []
                for r in range(reps):
                    s = state[now, r, at, :]
                    new = (
                        (a * state[now, r, above, :] + b * state[now, r, below, :])
                        + (c * state[now, r, before, :] + d * state[now, r, after, :])
                        + (centre * s + other * pltpu.roll(s, HALF, axis=1))
                    )
                    new = jnp.where(ocean, new, 0.0)
                    if k < STEPS - 1:
                        state[later, r, at, :] = new
                    else:
                        adj_ref[r, pl.ds(pl.multiple_of((x - REACH) * cols, 8) + j, 8), :] = new
                        if j in (0, cols - 8):
                            tiles[min(j, 1), r, pl.ds(pl.multiple_of((x - REACH) * 8, 8), 8), :] = new
                        news.append(new)
                if news:
                    sum_ref[pl.ds(pl.multiple_of((x - REACH) * cols, 8) + j, 8), :] = combine(coef_ref, news)
            return carry

        if k < STEPS - 1:
            sweep(row, k + 1, total - 2 * k - 2)

    stretch = rows // sems.shape[0]

    def out_copy(g):
        at = pl.ds(g * stretch * cols, stretch * cols)
        return pltpu.make_async_copy(adj_ref.at[:, at], adj_hbm.at[:, at], sems.at[g])

    def some_rows(g, carry):
        sweep(row, REACH + g * stretch, stretch)
        out_copy(g).start()
        return carry

    lax.fori_loop(0, sems.shape[0], some_rows, 0)
    for g in range(sems.shape[0]):
        out_copy(g).wait()


def edge_kernel(
    reps, rows, cols,
    coef_ref, edge_state, edge_terms, odd_ref, even_ref, tiles_in, adj_in, sum_in,
    tiles, adj_hbm, sum_ref,
    got, halo_state, halo_terms, state, spare, sems,
):
    del tiles_in, adj_in, sum_in
    strips, corners = y_index(reps)
    base = len(strips) * rows
    extra = spare.shape[0]

    def out_copy(side):
        target = adj_hbm.at[:, :, pl.ds(side * (cols - 8), 8)]
        return pltpu.make_async_copy(tiles.at[side].reshape(reps, rows, 8, 128), target, sems.at[side])

    parity = lax.rem(lax.axis_index("gy"), 2)
    got[0] = even_ref[...]
    got[1] = odd_ref[...]
    for side in (0, 1):
        source = got.at[1 - parity if side == 0 else parity]
        spare[...] = source[pl.ds(base, extra), :].astype(F32)

        def put(key, q, at, v, side=side):
            if key[0] == "f":
                halo_state[side, key[1], q, at, :] = v
            elif key[0] == 0:
                halo_terms[side, key[1], 0, q, at, :], halo_terms[side, key[1], 1, q, at, :] = speed_terms(v)
            else:
                halo_terms[side, key[1], 2, q, at, :], halo_terms[side, key[1], 3, q, at, :] = tracer_terms(v)

        for n, (key, d) in enumerate(strips):
            put(key, REACH - d, pl.ds(8 + REACH, rows), source[pl.ds(n * rows, rows), :].astype(F32))
        for n, (key, d, e, edge) in enumerate(corners):
            x = REACH - e if edge == 0 else REACH + rows + e - 1
            put(key, REACH - d, pl.ds(8 + x, 1), spare[pl.ds(n, 1), :])

        sign = 1.0 if side == 0 else -1.0

        def term(k, n, q, start, size, side=side):
            if q < REACH:
                return halo_terms[side, k, n, q, pl.ds(8 + start, size), :]
            return edge_terms[side, k, n, q - REACH, pl.ds(start, size), :]

        def cell(k, r, q, start, size, side=side):
            if k > 0:
                return state[(k - 1) % 2, r, q, pl.ds(8 + start, size), :]
            if q < REACH:
                return halo_state[side, r, q, pl.ds(8 + start, size), :]
            return edge_state[side, r, q - REACH, pl.ds(start, size), :]

        for k in range(STEPS):
            for q in range(k + 1, 8 - k):
                for start in range(k + 1, k + 1 + rows + 2 * (REACH - k - 1), 8):
                    size = min(8, k + 1 + rows + 2 * (REACH - k - 1) - start)
                    a = DT + term(k, 0, q, start - 1, size)
                    b = DT - term(k, 0, q, start + 1, size)
                    c = DT + sign * term(k, 1, q - 1, start, size)
                    d = DT - sign * term(k, 1, q + 1, start, size)
                    centre = term(k, 2, q, start, size)
                    other = term(k, 3, q, start, size)
                    ocean = centre < 1.0
                    news = []
                    for r in range(reps):
                        s = cell(k, r, q, start, size)
                        new = (
                            (a * cell(k, r, q, start - 1, size) + b * cell(k, r, q, start + 1, size))
                            + (c * cell(k, r, q - 1, start, size) + d * cell(k, r, q + 1, start, size))
                            + (centre * s + other * pltpu.roll(s, HALF, axis=1))
                        )
                        new = jnp.where(ocean, new, 0.0)
                        if k < STEPS - 1:
                            state[k % 2, r, q, pl.ds(8 + start, size), :] = new
                        news.append(new)
                    if k == STEPS - 1:
                        y = q - REACH if side == 0 else cols - 1 - (q - REACH)
                        sum_ref[pl.ds((start - REACH) * cols + y, size, stride=cols), :] = combine(coef_ref, news)
                        y = q - REACH if side == 0 else 7 - (q - REACH)
                        for r in range(reps):
                            tiles[side, r, pl.ds((start - REACH) * 8 + y, size, stride=8), :] = news[r]
        out_copy(side).start()
    for side in (0, 1):
        out_copy(side).wait()


def shift(x, axis, by):
    n = lax.axis_size(axis)
    if by > 0:
        return lax.ppermute(x, axis, [(i, i + 1) for i in range(n - 1)])
    return lax.ppermute(x, axis, [(i + 1, i) for i in range(n - 1)])


def local(velocity, tracers, forcing, coefficients, land_mask, step_levels):
    groups = lax.axis_size("rep")
    reps, rows, cols, lanes = forcing.shape
    own = rows // groups
    hbm = pl.BlockSpec(memory_space=pltpu.HBM)
    mine = pl.pallas_call(
        functools.partial(own_kernel, groups, own),
        out_shape=jax.ShapeDtypeStruct((groups, 2 * own, cols, lanes), BF16),
        in_specs=[hbm] * 3,
        scratch_shapes=[
            pltpu.VMEM(velocity.shape, BF16),
            pltpu.VMEM(tracers.shape, BF16),
            pltpu.VMEM(land_mask.shape, land_mask.dtype),
            pltpu.SemaphoreType.DMA((3,)),
        ],
        compiler_params=pltpu.CompilerParams(vmem_limit_bytes=8 * 2**20),
        name="own",
    )(*(pltpu.with_memory_space_constraint(x, pltpu.HBM) for x in (velocity, tracers, land_mask)))
    slices = lax.all_to_all(mine, "rep", 0, 0, tiled=True)
    slices, forcing, step_levels = lax.optimization_barrier((slices, forcing, step_levels))
    picked = pl.pallas_call(
        pick_kernel,
        out_shape=jax.ShapeDtypeStruct((STEPS, 2 * own, cols, lanes), BF16),
        in_specs=[pl.BlockSpec(memory_space=pltpu.SMEM), pl.BlockSpec(memory_space=pltpu.VMEM)],
        compiler_params=pltpu.CompilerParams(vmem_limit_bytes=8 * 2**20),
        name="pick",
    )(step_levels, slices)
    lev = lax.all_gather(picked.astype(jnp.float16), "rep", axis=0, tiled=False)
    lev = lax.optimization_barrier(lev).astype(BF16)

    def edge(rows_of, source):
        return [source[x // own, k, which * own + x % own] for which, k, x in rows_of]

    last, first = [], []
    for which, k, width in LEVEL_HALO:
        last += [(which, k, rows - width + i) for i in range(width)]
        first += [(which, k, i) for i in range(width)]
    to_down = jnp.concatenate([forcing[:, rows - REACH :].reshape(-1, cols, lanes), jnp.stack(edge(last, lev))])
    to_up = jnp.concatenate([forcing[:, :REACH].reshape(-1, cols, lanes), jnp.stack(edge(first, lev))])
    up = shift(to_down, "gx", 1)
    down = shift(to_up, "gx", -1)

    strips, corners = y_index(reps)
    extra = -(-len(corners) // 16) * 16
    length = len(strips) * rows + extra
    payload = jax.ShapeDtypeStruct((length, lanes), BF16)
    to_even, to_odd = pl.pallas_call(
        functools.partial(pack_kernel, reps, rows, cols),
        out_shape=(payload, payload),
        scratch_shapes=[
            pltpu.VMEM((2, length, lanes), BF16),
            pltpu.VMEM((rows * 8, lanes), F32),
            pltpu.VMEM((extra, lanes), F32),
        ],
        compiler_params=pltpu.CompilerParams(vmem_limit_bytes=8 * 2**20),
        name="pack",
    )(forcing, lev, up, down)
    odd = swaps(to_odd, "gy", 1)
    even = swaps(to_even, "gy", 0)

    vm = pl.BlockSpec(memory_space=pltpu.VMEM)
    sm = pl.BlockSpec(memory_space=pltpu.SMEM)
    size = (rows + 2 * REACH + 2) * cols
    total = jax.ShapeDtypeStruct((rows * cols, lanes), F32)
    tiled = jax.ShapeDtypeStruct((2, reps, rows * 8, lanes), F32)
    adjoints, weighted, edge_state, edge_terms, tiles = pl.pallas_call(
        functools.partial(inner_kernel, reps, rows, cols),
        out_shape=(
            jax.ShapeDtypeStruct((reps, rows * cols, lanes), F32),
            total,
            jax.ShapeDtypeStruct((2, reps, DEEP, TALL, lanes), F32),
            jax.ShapeDtypeStruct((2, STEPS, 4, DEEP, TALL, lanes), F32),
            tiled,
        ),
        in_specs=[sm] + [vm] * 4,
        out_specs=(hbm,) + (vm,) * 4,
        scratch_shapes=[pltpu.VMEM((2, reps, size, lanes), F32)]
        + [pltpu.VMEM((size, lanes), F32)] * 4
        + [pltpu.VMEM((reps, rows * cols, lanes), F32), pltpu.SemaphoreType.DMA((4,))],
        compiler_params=pltpu.CompilerParams(vmem_limit_bytes=24 * 2**20),
        name="inner",
    )(coefficients, forcing, lev, up, down)
    adjoints = adjoints.reshape(reps, rows, cols, lanes)
    long = 8 + TALL + 2
    _, adjoints, weighted = pl.pallas_call(
        functools.partial(edge_kernel, reps, rows, cols),
        out_shape=(tiled, jax.ShapeDtypeStruct(adjoints.shape, F32), total),
        in_specs=[sm] + [vm] * 5 + [hbm, vm],
        out_specs=(vm, hbm, vm),
        scratch_shapes=[
            pltpu.VMEM((2, length, lanes), BF16),
            pltpu.VMEM((2, reps, REACH, long, lanes), F32),
            pltpu.VMEM((2, STEPS, 4, REACH, long, lanes), F32),
            pltpu.VMEM((2, reps, REACH + DEEP, long, lanes), F32),
            pltpu.VMEM((extra, lanes), F32),
            pltpu.SemaphoreType.DMA((2,)),
        ],
        input_output_aliases={5: 0, 6: 1, 7: 2},
        compiler_params=pltpu.CompilerParams(vmem_limit_bytes=12 * 2**20),
        name="edge",
    )(coefficients, edge_state, edge_terms, odd, even, tiles, adjoints, weighted)

    parts = lax.all_to_all(weighted.reshape(groups, own, cols, lanes), "rep", 0, 0, tiled=True)
    return jnp.sum(parts, axis=0), adjoints


def solution(mesh):
    placed = (
        P("rep", "gx", "gy", None),
        P("rep", "gx", "gy", None),
        P("rep", "gx", "gy", None),
        P("rep"),
        P("gx", "gy"),
        P(),
    )
    return jax.shard_map(
        local,
        mesh=mesh,
        in_specs=placed,
        out_specs=(P(("gx", "rep"), "gy", None), P("rep", "gx", "gy", None)),
        check_vma=False,
    )
```

```python
import functools

import jax
import jax.numpy as jnp
from jax import lax
from jax.experimental import pallas as pl
from jax.experimental.pallas import tpu as pltpu
from jax.sharding import PartitionSpec as P

F32 = jnp.float32
BF16 = jnp.bfloat16
STEPS = 3
REACH = 3
SCALE = 2.0**15
DT = 0.1
HALF = 64
LAND = 4.0
TALL = 38
DEEP = 6

LEVEL_HALO = ((0, 0, 3), (1, 0, 2), (0, 1, 2), (1, 1, 1), (0, 2, 1))


def x_index(reps):
    table, at = {}, 0
    for r in range(reps):
        table["f", r] = (at, REACH)
        at += REACH
    for which, level, width in LEVEL_HALO:
        table[which, level] = (at, width)
        at += width
    return table, at


def y_index(reps):
    keys = [("f", r) for r in range(reps)] + [(w, k) for w, k, _ in LEVEL_HALO]
    width = {("f", r): REACH for r in range(reps)}
    width.update({(w, k): n for w, k, n in LEVEL_HALO})
    strips = [(key, d) for key in keys for d in range(1, width[key] + 1)]
    corners = [
        (key, d, e, side)
        for key in keys
        for d in range(1, width[key])
        for e in range(1, width[key] - d + 1)
        for side in (0, 1)
    ]
    return strips, corners


def swaps(x, axis, first):
    ends = lax.axis_size(axis) - 1
    return lax.ppermute(x, axis, [p for i in range(first, ends, 2) for p in ((i, i + 1), (i + 1, i))])


def pack_kernel(reps, rows, cols, f_ref, lev_ref, up_ref, down_ref, even_ref, odd_ref, both, tile, out):
    xi, _ = x_index(reps)
    strips, corners = y_index(reps)
    keys = []
    for key, _ in strips:
        if key not in keys:
            keys.append(key)
    base = len(strips) * rows
    for side in (0, 1):
        target = both.at[side]
        lo = 0 if side == 0 else cols - 8
        for key in keys:
            for x in range(rows):
                if key[0] == "f":
                    v = f_ref[key[1], x, lo : lo + 8, :]
                else:
                    v = lev_ref[x // 2, key[1], 2 * key[0] + x % 2, lo : lo + 8, :]
                tile[pl.ds(x * 8, 8), :] = v.astype(F32)
            for n, (k, d) in enumerate(strips):
                if k == key:
                    c = d - 1 if side == 0 else 8 - d
                    target[pl.ds(n * rows, rows), :] = tile[pl.ds(c, rows, stride=8), :].astype(target.dtype)
        out[...] = jnp.zeros_like(out)
        for n, (key, d, e, edge) in enumerate(corners):
            first, width = xi[key]
            row = up_ref[first + width - e, lo : lo + 8, :] if edge == 0 else down_ref[first + e - 1, lo : lo + 8, :]
            c = d - 1 if side == 0 else 8 - d
            out[pl.ds(n, 1), :] = row.astype(F32)[c : c + 1]
        target[pl.ds(base, out.shape[0]), :] = out[...].astype(target.dtype)
    parity = lax.rem(lax.axis_index("gy"), 2)
    even_ref[...] = both[1 - parity]
    odd_ref[...] = both[parity]


def own_kernel(groups, own, v_hbm, t_hbm, mask_hbm, out, v_ref, t_ref, mask_ref, sems):
    copies = [
        pltpu.make_async_copy(source, target, sems.at[n])
        for n, (source, target) in enumerate(((mask_hbm, mask_ref), (v_hbm, v_ref), (t_hbm, t_ref)))
    ]
    for copy in copies:
        copy.start()
    copies[0].wait()
    ocean = jnp.transpose(mask_ref[...].astype(F32))
    copies[1].wait()
    for x in range(groups * own):
        out[x // own, x % own] = v_ref[0, x] * BF16(SCALE)
    copies[2].wait()
    for x in range(groups * own):
        t = t_ref[0, x].astype(F32)
        out[x // own, own + x % own] = jnp.where(ocean[:, x : x + 1] > 0.0, t, 0.0).astype(BF16)


def pick_kernel(levels_ref, slices_ref, out):
    for k in range(STEPS):
        out[k] = slices_ref[levels_ref[k]]


def combine(coef_ref, news):
    total = None
    for r, new in enumerate(news):
        part = coef_ref[r] * new
        total = part if total is None else total + part
    return total


def speed_terms(v):
    v = v * (0.5 * DT / SCALE)
    o = pltpu.roll(v, HALF, axis=1)
    low = lax.broadcasted_iota(jnp.int32, v.shape, 1) < HALF
    return jnp.where(low, v, o), jnp.where(low, o, v)


def tracer_terms(t):
    return jnp.where(t > 0.0, (1.0 - 4.0 * DT) - DT * t, LAND), DT * pltpu.roll(t, HALF, axis=1)


def edge_columns(k):
    return (5 - k, 6 - k, 5 - k, 5 - k)


def sweep(body, start, count, by=8):
    def several(g, carry):
        for i in range(by):
            body(start + g * by + i, carry)
        return carry

    lax.fori_loop(0, count // by, several, 0)
    for i in range(count // by * by, count):
        body(start + i, 0)


def inner_kernel(
    reps, rows, cols,
    coef_ref, f_ref, lev_ref, up_ref, down_ref,
    adj_hbm, sum_ref, edge_state, edge_terms, tiles,
    state, vx, vy, keep, swap, adj_ref, sems,
):
    xi, _ = x_index(reps)
    total = rows + 2 * REACH
    own = lev_ref.shape[2] // 2

    def slot(x):
        return pl.ds(pl.multiple_of((x + 1) * cols, 8), cols)

    def put_speed(x, v):
        vx[slot(x), :], vy[slot(x), :] = speed_terms(v)

    def put_tracer(x, t):
        keep[slot(x), :], swap[slot(x), :] = tracer_terms(t)

    def put_rows(put, key):
        if key in xi:
            first, width = xi[key]
            for e in range(1, width + 1):
                put(REACH - e, up_ref[first + width - e].astype(F32))
                put(REACH + rows + e - 1, down_ref[first + e - 1].astype(F32))

    def forcing_row(x, carry):
        for r in range(reps):
            state[0, r, slot(x + REACH), :] = f_ref[r, x].astype(F32)
        return carry

    lax.fori_loop(0, rows, forcing_row, 0, unroll=4)
    for r in range(reps):

        def put_state(x, v, r=r):
            state[0, r, slot(x), :] = v

        put_rows(put_state, ("f", r))
        for side in (0, 1):
            for depth in range(edge_state.shape[2]):
                y = depth if side == 0 else cols - 1 - depth
                edge_state[side, r, depth] = state[0, r, pl.ds(cols + y, TALL, stride=cols), :]

    for k in range(STEPS):
        now, later = k % 2, (k + 1) % 2

        def level_rows(g, carry, k=k):
            for i in range(own):
                put_speed(g * own + i + REACH, lev_ref[g, k, i].astype(F32))
                put_tracer(g * own + i + REACH, lev_ref[g, k, own + i].astype(F32))
            return carry

        lax.fori_loop(0, lev_ref.shape[0], level_rows, 0, unroll=4)
        put_rows(put_speed, (0, k))
        put_rows(put_tracer, (1, k))
        for side in (0, 1):
            for n, (source, count) in enumerate(zip((vx, vy, keep, swap), edge_columns(k))):
                for depth in range(count):
                    y = depth if side == 0 else cols - 1 - depth
                    edge_terms[side, k, n, depth] = source[pl.ds(cols + y, TALL, stride=cols), :]

        def row(x, carry, k=k, now=now, later=later):
            start = pl.multiple_of((x + 1) * cols, 8)
            for j in range(0, cols, 8):
                at = pl.ds(start + j, 8)
                above, below = pl.ds(start + j - cols, 8), pl.ds(start + j + cols, 8)
                before, after = pl.ds(start + j - 1, 8), pl.ds(start + j + 1, 8)
                a = DT + vx[above, :]
                b = DT - vx[below, :]
                c = DT + vy[before, :]
                d = DT - vy[after, :]
                centre = keep[at, :]
                other = swap[at, :]
                ocean = centre < 1.0
                news = []
                for r in range(reps):
                    s = state[now, r, at, :]
                    new = (
                        (a * state[now, r, above, :] + b * state[now, r, below, :])
                        + (c * state[now, r, before, :] + d * state[now, r, after, :])
                        + (centre * s + other * pltpu.roll(s, HALF, axis=1))
                    )
                    new = jnp.where(ocean, new, 0.0)
                    if k < STEPS - 1:
                        state[later, r, at, :] = new
                    else:
                        adj_ref[r, pl.ds(pl.multiple_of((x - REACH) * cols, 8) + j, 8), :] = new
                        if j in (0, cols - 8):
                            tiles[min(j, 1), r, pl.ds(pl.multiple_of((x - REACH) * 8, 8), 8), :] = new
                        news.append(new)
                if news:
                    sum_ref[pl.ds(pl.multiple_of((x - REACH) * cols, 8) + j, 8), :] = combine(coef_ref, news)
            return carry

        if k < STEPS - 1:
            sweep(row, k + 1, total - 2 * k - 2)

    stretch = rows // sems.shape[0]

    def out_copy(g):
        at = pl.ds(g * stretch * cols, stretch * cols)
        return pltpu.make_async_copy(adj_ref.at[:, at], adj_hbm.at[:, at], sems.at[g])

    def some_rows(g, carry):
        sweep(row, REACH + g * stretch, stretch)
        out_copy(g).start()
        return carry

    lax.fori_loop(0, sems.shape[0], some_rows, 0)
    for g in range(sems.shape[0]):
        out_copy(g).wait()


def edge_kernel(
    reps, rows, cols,
    coef_ref, edge_state, edge_terms, even_ref, odd_ref, tiles_in, adj_in, sum_in,
    tiles, adj_hbm, sum_ref,
    got, halo_state, halo_terms, state, spare, sems,
):
    del tiles_in, adj_in, sum_in
    strips, corners = y_index(reps)
    base = len(strips) * rows
    extra = spare.shape[0]

    def out_copy(side):
        target = adj_hbm.at[:, :, pl.ds(side * (cols - 8), 8)]
        return pltpu.make_async_copy(tiles.at[side].reshape(reps, rows, 8, 128), target, sems.at[side])

    parity = lax.rem(lax.axis_index("gy"), 2)
    got[0] = even_ref[...]
    got[1] = odd_ref[...]
    for side in (0, 1):
        source = got.at[1 - parity if side == 0 else parity]
        spare[...] = source[pl.ds(base, extra), :].astype(F32)

        def put(key, q, at, v, side=side):
            if key[0] == "f":
                halo_state[side, key[1], q, at, :] = v
            elif key[0] == 0:
                halo_terms[side, key[1], 0, q, at, :], halo_terms[side, key[1], 1, q, at, :] = speed_terms(v)
            else:
                halo_terms[side, key[1], 2, q, at, :], halo_terms[side, key[1], 3, q, at, :] = tracer_terms(v)

        for n, (key, d) in enumerate(strips):
            put(key, REACH - d, pl.ds(8 + REACH, rows), source[pl.ds(n * rows, rows), :].astype(F32))
        for n, (key, d, e, edge) in enumerate(corners):
            x = REACH - e if edge == 0 else REACH + rows + e - 1
            put(key, REACH - d, pl.ds(8 + x, 1), spare[pl.ds(n, 1), :])

        sign = 1.0 if side == 0 else -1.0

        def term(k, n, q, start, size, side=side):
            if q < REACH:
                return halo_terms[side, k, n, q, pl.ds(8 + start, size), :]
            return edge_terms[side, k, n, q - REACH, pl.ds(start, size), :]

        def cell(k, r, q, start, size, side=side):
            if k > 0:
                return state[(k - 1) % 2, r, q, pl.ds(8 + start, size), :]
            if q < REACH:
                return halo_state[side, r, q, pl.ds(8 + start, size), :]
            return edge_state[side, r, q - REACH, pl.ds(start, size), :]

        for k in range(STEPS):
            for q in range(k + 1, 8 - k):
                for start in range(k + 1, k + 1 + rows + 2 * (REACH - k - 1), 8):
                    size = min(8, k + 1 + rows + 2 * (REACH - k - 1) - start)
                    a = DT + term(k, 0, q, start - 1, size)
                    b = DT - term(k, 0, q, start + 1, size)
                    c = DT + sign * term(k, 1, q - 1, start, size)
                    d = DT - sign * term(k, 1, q + 1, start, size)
                    centre = term(k, 2, q, start, size)
                    other = term(k, 3, q, start, size)
                    ocean = centre < 1.0
                    news = []
                    for r in range(reps):
                        s = cell(k, r, q, start, size)
                        new = (
                            (a * cell(k, r, q, start - 1, size) + b * cell(k, r, q, start + 1, size))
                            + (c * cell(k, r, q - 1, start, size) + d * cell(k, r, q + 1, start, size))
                            + (centre * s + other * pltpu.roll(s, HALF, axis=1))
                        )
                        new = jnp.where(ocean, new, 0.0)
                        if k < STEPS - 1:
                            state[k % 2, r, q, pl.ds(8 + start, size), :] = new
                        news.append(new)
                    if k == STEPS - 1:
                        y = q - REACH if side == 0 else cols - 1 - (q - REACH)
                        sum_ref[pl.ds((start - REACH) * cols + y, size, stride=cols), :] = combine(coef_ref, news)
                        y = q - REACH if side == 0 else 7 - (q - REACH)
                        for r in range(reps):
                            tiles[side, r, pl.ds((start - REACH) * 8 + y, size, stride=8), :] = news[r]
        out_copy(side).start()
    for side in (0, 1):
        out_copy(side).wait()


def shift(x, axis, by):
    n = lax.axis_size(axis)
    if by > 0:
        return lax.ppermute(x, axis, [(i, i + 1) for i in range(n - 1)])
    return lax.ppermute(x, axis, [(i + 1, i) for i in range(n - 1)])


def local(velocity, tracers, forcing, coefficients, land_mask, step_levels):
    groups = lax.axis_size("rep")
    reps, rows, cols, lanes = forcing.shape
    own = rows // groups
    hbm = pl.BlockSpec(memory_space=pltpu.HBM)
    mine = pl.pallas_call(
        functools.partial(own_kernel, groups, own),
        out_shape=jax.ShapeDtypeStruct((groups, 2 * own, cols, lanes), BF16),
        in_specs=[hbm] * 3,
        scratch_shapes=[
            pltpu.VMEM(velocity.shape, BF16),
            pltpu.VMEM(tracers.shape, BF16),
            pltpu.VMEM(land_mask.shape, land_mask.dtype),
            pltpu.SemaphoreType.DMA((3,)),
        ],
        compiler_params=pltpu.CompilerParams(vmem_limit_bytes=8 * 2**20),
        name="own",
    )(*(pltpu.with_memory_space_constraint(x, pltpu.HBM) for x in (velocity, tracers, land_mask)))
    slices = lax.all_to_all(mine, "rep", 0, 0, tiled=True)
    slices, forcing, step_levels = lax.optimization_barrier((slices, forcing, step_levels))
    picked = pl.pallas_call(
        pick_kernel,
        out_shape=jax.ShapeDtypeStruct((STEPS, 2 * own, cols, lanes), BF16),
        in_specs=[pl.BlockSpec(memory_space=pltpu.SMEM), pl.BlockSpec(memory_space=pltpu.VMEM)],
        compiler_params=pltpu.CompilerParams(vmem_limit_bytes=8 * 2**20),
        name="pick",
    )(step_levels, slices)
    lev = lax.all_gather(picked.astype(jnp.float16), "rep", axis=0, tiled=False)
    lev = lax.optimization_barrier(lev).astype(BF16)

    def edge(rows_of, source):
        return [source[x // own, k, which * own + x % own] for which, k, x in rows_of]

    last, first = [], []
    for which, k, width in LEVEL_HALO:
        last += [(which, k, rows - width + i) for i in range(width)]
        first += [(which, k, i) for i in range(width)]
    to_down = jnp.concatenate([forcing[:, rows - REACH :].reshape(-1, cols, lanes), jnp.stack(edge(last, lev))])
    to_up = jnp.concatenate([forcing[:, :REACH].reshape(-1, cols, lanes), jnp.stack(edge(first, lev))])
    up = shift(to_down, "gx", 1)
    down = shift(to_up, "gx", -1)

    strips, corners = y_index(reps)
    extra = -(-len(corners) // 16) * 16
    length = len(strips) * rows + extra
    payload = jax.ShapeDtypeStruct((length, lanes), BF16)
    to_even, to_odd = pl.pallas_call(
        functools.partial(pack_kernel, reps, rows, cols),
        out_shape=(payload, payload),
        scratch_shapes=[
            pltpu.VMEM((2, length, lanes), BF16),
            pltpu.VMEM((rows * 8, lanes), F32),
            pltpu.VMEM((extra, lanes), F32),
        ],
        compiler_params=pltpu.CompilerParams(vmem_limit_bytes=8 * 2**20),
        name="pack",
    )(forcing, lev, up, down)
    odd = swaps(to_odd, "gy", 1)
    even = swaps(to_even, "gy", 0)

    vm = pl.BlockSpec(memory_space=pltpu.VMEM)
    sm = pl.BlockSpec(memory_space=pltpu.SMEM)
    size = (rows + 2 * REACH + 2) * cols
    total = jax.ShapeDtypeStruct((rows * cols, lanes), F32)
    tiled = jax.ShapeDtypeStruct((2, reps, rows * 8, lanes), F32)
    adjoints, weighted, edge_state, edge_terms, tiles = pl.pallas_call(
        functools.partial(inner_kernel, reps, rows, cols),
        out_shape=(
            jax.ShapeDtypeStruct((reps, rows * cols, lanes), F32),
            total,
            jax.ShapeDtypeStruct((2, reps, DEEP, TALL, lanes), F32),
            jax.ShapeDtypeStruct((2, STEPS, 4, DEEP, TALL, lanes), F32),
            tiled,
        ),
        in_specs=[sm] + [vm] * 4,
        out_specs=(hbm,) + (vm,) * 4,
        scratch_shapes=[pltpu.VMEM((2, reps, size, lanes), F32)]
        + [pltpu.VMEM((size, lanes), F32)] * 4
        + [pltpu.VMEM((reps, rows * cols, lanes), F32), pltpu.SemaphoreType.DMA((4,))],
        compiler_params=pltpu.CompilerParams(vmem_limit_bytes=24 * 2**20),
        name="inner",
    )(coefficients, forcing, lev, up, down)
    adjoints = adjoints.reshape(reps, rows, cols, lanes)
    long = 8 + TALL + 2
    _, adjoints, weighted = pl.pallas_call(
        functools.partial(edge_kernel, reps, rows, cols),
        out_shape=(tiled, jax.ShapeDtypeStruct(adjoints.shape, F32), total),
        in_specs=[sm] + [vm] * 5 + [hbm, vm],
        out_specs=(vm, hbm, vm),
        scratch_shapes=[
            pltpu.VMEM((2, length, lanes), BF16),
            pltpu.VMEM((2, reps, REACH, long, lanes), F32),
            pltpu.VMEM((2, STEPS, 4, REACH, long, lanes), F32),
            pltpu.VMEM((2, reps, REACH + DEEP, long, lanes), F32),
            pltpu.VMEM((extra, lanes), F32),
            pltpu.SemaphoreType.DMA((2,)),
        ],
        input_output_aliases={5: 0, 6: 1, 7: 2},
        compiler_params=pltpu.CompilerParams(vmem_limit_bytes=12 * 2**20),
        name="edge",
    )(coefficients, edge_state, edge_terms, even, odd, tiles, adjoints, weighted)

    parts = lax.all_to_all(weighted.reshape(groups, own, cols, lanes), "rep", 0, 0, tiled=True)
    return jnp.sum(parts, axis=0), adjoints


def solution(mesh):
    placed = (
        P("rep", "gx", "gy", None),
        P("rep", "gx", "gy", None),
        P("rep", "gx", "gy", None),
        P("rep"),
        P("gx", "gy"),
        P(),
    )
    return jax.shard_map(
        local,
        mesh=mesh,
        in_specs=placed,
        out_specs=(P(("gx", "rep"), "gy", None), P("rep", "gx", "gy", None)),
        check_vma=False,
    )
```
